32 devices in a mesh: gx: 2 (over x), gy: 16 (over z, y, core).
Axes of the slice: x: 2, y: 2, z: 4, core: 2. Of those that a mesh axis runs over, the one named last changes fastest.
Arguments:
- offsets: float32 [3, 4, 32, 2, 128], P(None, 'gx', 'gy'), may hold values from 0 to 1
- velocity: float32 [3, 4, 32, 2, 128], P(None, 'gx', 'gy'), may hold values from -6 to 6
- mass: float32 [4, 32, 2, 128], P('gx', 'gy'), may hold values from 0.00390625 to 0.03125
- energy: float32 [4, 32, 2, 128], P('gx', 'gy'), may hold values from 0.3 to 3
- counts: int32 [4, 32, 2], P('gx', 'gy'), may hold values from 1 to 128
Outputs:
- density: float32 [4, 32, 2, 128], P('gx', 'gy')
- acceleration: float32 [3, 4, 32, 2, 128], P(None, 'gx', 'gy')
- heating: float32 [4, 32, 2, 128], P('gx', 'gy')
The draws below stay inside these ranges and needn't reach their ends.
Inputs may be any that keep to these rules, and one draw needn't show every extreme that they name: Slots of a cell from counts on hold no particle.
All inputs are finite; a program needn't handle non-finite values.
Results may differ from the reference program's by a relative error of at most 0.0003.
Values sent between devices are 32-bit elements; how exact they have to be, the bound alone decides.
A program may use at most 64 MiB of HBM per device.

```python
import math
import jax
import jax.numpy as jnp
from jax import lax

P_SIZE = 128
CZ = 2
NX = 4
NY = 32


def set_ends(values, own_key, smallest, top_value):
    spot = [jax.random.randint(jax.random.fold_in(own_key, axis), (), 0, length) for axis, length in enumerate(values.shape)]
    widest = values.shape.index(max(values.shape))
    next_to = spot[:widest] + [(spot[widest] + 1) % values.shape[widest]] + spot[widest + 1:]
    return values.at[tuple(spot)].set(smallest).at[tuple(next_to)].set(top_value)


def steps_of(stream_key, shape, shards, low, top_value):
    factor_of = 1.0
    for dim, shards_of in shards:
        draws = jax.random.uniform(jax.random.fold_in(jax.random.fold_in(stream_key, 6), dim), (shards_of,), jnp.float32, low / len(shards), top_value / len(shards))
        factor_of = factor_of * jnp.repeat(jnp.exp(draws), shape[dim] // shards_of).reshape((-1,) + (1,) * (len(shape) - 1 - dim))
    return factor_of


def normal_values(own_key, extent, deviation, bound, pieces=(), kind=jnp.bfloat16):
    entries = jax.random.normal(own_key, extent, jnp.float32) * deviation
    if len(pieces) > 0:
        entries = steps_of(own_key, extent, pieces, -0.22, 0.18) * entries
    return jnp.clip(entries, min=-bound, max=bound).astype(kind)


def setup_inputs(seed: int = 0) -> dict:
    seeds = jax.random.split(jax.random.key(seed), 6)
    return {
        "offsets": jnp.clip(1.0 * jax.random.uniform(seeds[0], (3, NX, NY, CZ, P_SIZE), jnp.float32) ** steps_of(seeds[0], (3, NX, NY, CZ, P_SIZE), ((1, 2), (2, 16)), -0.2, 0.2), 0.0, 1.0),
        "velocity": normal_values(seeds[1], (3, NX, NY, CZ, P_SIZE), 1.0, 6.0, ((1, 2), (2, 16)), jnp.float32),
        "mass": jnp.clip(jnp.exp(math.log(0.03125) - 2.0794415 * jax.random.uniform(seeds[2], (NX, NY, CZ, P_SIZE), jnp.float32) ** steps_of(seeds[2], (NX, NY, CZ, P_SIZE), ((0, 2), (1, 16)), -0.2, 0.2)), 0.00390625, 0.03125),
        "energy": jnp.clip(jnp.exp(math.log(3.0) - 2.3025851 * jax.random.uniform(seeds[3], (NX, NY, CZ, P_SIZE), jnp.float32) ** steps_of(seeds[3], (NX, NY, CZ, P_SIZE), ((0, 2), (1, 16)), -0.2, 0.2)), 0.3, 3.0),
        "counts": set_ends(jax.random.randint(seeds[4], (NX, NY, CZ), 1, P_SIZE + 1), jax.random.fold_in(seeds[4], 1), 1, P_SIZE).astype(jnp.int32),
    }


SMOOTHING = 0.5
NORMALISE = 1.0 / (math.pi * 0.125)
ADIABATIC = 5.0 / 3.0
VISC_ALPHA = 1.0
VISC_BETA = 2.0
SOFTENING = 0.01

def offsets_list():
    result = []
    for shift_x in (-1, 0, 1):
        for shift_y in (-1, 0, 1):
            for shift_z in (-1, 0, 1):
                result.append((shift_x, shift_y, shift_z))
    return result

def density_terms(own_cell, near_cell, delta):
    step = jnp.asarray(delta, jnp.float32).reshape(3, 1, 1, 1)
    separation = own_cell[0:3, :, :, None] - near_cell[0:3, :, None, :] - step
    scaled = jnp.sqrt(lax.optimization_barrier(jnp.sum(separation * separation, axis=0))) / SMOOTHING
    outer = jnp.maximum(2.0 - scaled, 0.0)
    inner = jnp.maximum(1.0 - scaled, 0.0)
    kernel = NORMALISE * (0.25 * outer * outer * outer - inner * inner * inner)
    return lax.optimization_barrier(jnp.sum(kernel * near_cell[6][:, None, :], axis=-1))

def force_terms(own_cell, near_cell, delta):
    step = jnp.asarray(delta, jnp.float32).reshape(3, 1, 1, 1)
    separation = own_cell[0:3, :, :, None] - near_cell[0:3, :, None, :] - step
    relative = own_cell[3:6, :, :, None] - near_cell[3:6, :, None, :]
    distance_sq = lax.optimization_barrier(jnp.sum(separation * separation, axis=0))
    scaled = jnp.sqrt(distance_sq) / SMOOTHING
    safe_scaled = jnp.where(scaled < 1.0, 1.0, scaled)
    outer = jnp.maximum(2.0 - scaled, 0.0)
    slope = jnp.where(scaled < 1.0, -3.0 + 2.25 * scaled, -0.75 * outer * outer / safe_scaled)
    weight = near_cell[6][:, None, :] * (NORMALISE / (SMOOTHING * SMOOTHING)) * slope
    approach = lax.optimization_barrier(jnp.sum(relative * separation, axis=0))
    closing = SMOOTHING * jnp.minimum(approach, 0.0) / (distance_sq + SOFTENING * SMOOTHING * SMOOTHING)
    sound = 0.5 * (own_cell[8][:, :, None] + near_cell[8][:, None, :])
    mean_rho = 0.5 * (own_cell[9][:, :, None] + near_cell[9][:, None, :])
    viscous = (-VISC_ALPHA * sound * closing + VISC_BETA * closing * closing) / mean_rho
    pushing = weight * (own_cell[7][:, :, None] + near_cell[7][:, None, :] + viscous)
    accel = -lax.optimization_barrier(jnp.sum(pushing[None] * separation, axis=-1))
    heat = lax.optimization_barrier(jnp.sum(weight * (own_cell[7][:, :, None] + 0.5 * viscous) * approach, axis=-1))
    return jnp.concatenate([accel, heat[None]], axis=0)

def block_apply(extended, count_x, count_y, terms, rows_out):
    layers = extended.shape[3] - 2
    slots = extended.shape[4]

    def column(position):
        first = position // count_y
        second = position % count_y
        zero = jnp.zeros((), jnp.int32)
        neighbours = lax.dynamic_slice(extended, (zero, first, second, zero, zero), (extended.shape[0], 3, 3, layers + 2, slots))
        own_cell = neighbours[:, 1, 1, 1:layers + 1]
        total = jnp.zeros((rows_out, layers, slots), jnp.float32)
        for delta in offsets_list():
            near_cell = neighbours[:, 1 + delta[0], 1 + delta[1], 1 + delta[2]:1 + delta[2] + layers]
            total = total + terms(own_cell, near_cell, delta).reshape(rows_out, layers, slots)
        return total
    columns = lax.map(column, jnp.arange(count_x * count_y, dtype=jnp.int32))
    columns = columns.reshape(count_x, count_y, rows_out, layers, slots)
    return jnp.moveaxis(columns, 2, 0)

def force_inputs(particles, density_safe):
    energy_part = particles[7]
    pressure_term = (ADIABATIC - 1.0) * energy_part / density_safe
    sound = jnp.sqrt(ADIABATIC * (ADIABATIC - 1.0) * energy_part)
    return jnp.concatenate([particles[0:7], pressure_term[None], sound[None], density_safe[None]], axis=0)

def reference(offsets, velocity, mass, energy, counts):
    slots = mass.shape[-1]
    occupied = (jnp.arange(slots, dtype=jnp.int32)[None, None, None, :] < counts[..., None]).astype(jnp.float32)
    particles = jnp.concatenate([offsets, velocity, (mass * occupied)[None], energy[None]], axis=0)
    extended = jnp.pad(particles, ((0, 0), (1, 1), (1, 1), (0, 0), (0, 0)), mode='wrap')
    extended = jnp.pad(extended, ((0, 0), (0, 0), (0, 0), (1, 1), (0, 0)))
    count_x = mass.shape[0]
    count_y = mass.shape[1]
    density = block_apply(extended, count_x, count_y, density_terms, 1)[0]
    density_safe = jnp.where(particles[6] > 0.0, density, 1.0)
    density_wide = jnp.pad(density_safe, ((1, 1), (1, 1), (0, 0), (0, 0)), mode='wrap')
    density_wide = jnp.pad(density_wide, ((0, 0), (0, 0), (1, 1), (0, 0)), constant_values=1.0)
    forces = block_apply(force_inputs(extended, density_wide), count_x, count_y, force_terms, 4)
    return (density * occupied, forces[0:3] * occupied[None], forces[3] * occupied)
```

```python
import functools
import math

import jax
import jax.numpy as jnp
from jax import lax
from jax.experimental import pallas as pl
from jax.experimental.pallas import tpu as pltpu
from jax.sharding import PartitionSpec as P

SMOOTHING = 0.5
NORMALISE = 1.0 / (math.pi * 0.125)
ADIABATIC = 5.0 / 3.0
VISC_ALPHA = 1.0
VISC_BETA = 2.0
SOFTENING = 0.01
TINY = 1e-30
VMEM = pltpu.VMEM
MESH = pl.DeviceIdType.MESH
DIRECTIONS = [(dx, dy) for dx in (-1, 0, 1) for dy in (-1, 0, 1) if (dx, dy) != (0, 0)]
RAW = 56
DEPTH = 64
THERMAL = 64
SUMS = 5


def edge(step, count):
    if step == 0:
        return (0, 1, count)
    if step == 1:
        return (count - 1, 0, 1)
    return (0, count + 1, 1)


def start_copies(peers, own_ref, out_ref, count_x, count_y, send_sem, recv_sem):
    copies = []
    for k, (dx, dy) in enumerate(DIRECTIONS):
        from_x, to_x, width_x = edge(dx, count_x)
        from_y, to_y, width_y = edge(dy, count_y)
        copy = pltpu.make_async_remote_copy(
            src_ref=own_ref.at[pl.ds(from_x, width_x), pl.ds(from_y, width_y)],
            dst_ref=out_ref.at[pl.ds(to_x, width_x), pl.ds(to_y, width_y)],
            send_sem=send_sem.at[k],
            recv_sem=recv_sem.at[k],
            device_id=peers[k],
            device_id_type=MESH,
        )
        copy.start()
        copies.append(copy)
    return copies


def split(values):
    high = values.astype(jnp.bfloat16).astype(jnp.float32)
    rest = values - high
    middle = rest.astype(jnp.bfloat16).astype(jnp.float32)
    return high, middle, rest - middle


def look_up(step, values):
    result = step + values[0]
    for k in range(1, len(values)):
        jump = values[k] - values[k - 1] - 1
        if jump:
            result = result + jnp.where(step >= k, jump, 0)
    return result


def fold(values):
    return jnp.sum(values.reshape(values.shape[0] // 8, 8, values.shape[1]), axis=0)


def thermal_rows(energy, rho):
    pressure = (ADIABATIC - 1.0) * energy / rho
    sound = jnp.sqrt(ADIABATIC * (ADIABATIC - 1.0) * energy) * (0.5 * VISC_ALPHA / VISC_BETA)
    dense = rho * (0.5 / VISC_BETA)
    rows = lax.broadcasted_iota(jnp.int32, (8, energy.shape[1]), 0)
    return jnp.where(rows == 0, pressure, jnp.where(rows == 1, sound, jnp.where(rows == 2, dense, 0.0)))


def sph_kernel(
    size_gx, size_gy, offsets_hbm, velocity_hbm, mass_hbm, energy_hbm, counts_ref,
    density_out, accel_out, heat_out,
    offsets_ref, velocity_ref, mass_ref, energy_ref, own_ref, ext_ref, safe_ref, near_ref,
    list_ref, left_ref, right_ref, mine_ref, total_ref, sums_ref, dist_ref, pair_ref,
    send_sem, recv_sem, rho_send, rho_recv, in_sem,
):
    count_x, count_y, layers, _, slots = own_ref.shape
    size_y = count_y + 2
    span = layers * slots
    own = [(x, y) for x in range(1, count_x + 1) for y in range(1, count_y + 1)]
    my_x, my_y = lax.axis_index("gx"), lax.axis_index("gy")
    barrier = pltpu.get_barrier_semaphore()
    peers = []
    for dx, dy in DIRECTIONS:
        peers.append(
            (lax.rem(my_x + dx + size_gx, size_gx), lax.rem(my_y + dy + size_gy, size_gy))
        )
    for peer in peers:
        pl.semaphore_signal(barrier, inc=1, device_id=peer, device_id_type=MESH)
    sources = (offsets_hbm, velocity_hbm, mass_hbm, energy_hbm)
    targets = (offsets_ref, velocity_ref, mass_ref, energy_ref)
    loads = [pltpu.make_async_copy(a, b, in_sem.at[k]) for k, (a, b) in enumerate(zip(sources, targets))]
    for load in loads:
        load.start()
    for load in loads:
        load.wait()
    lane = lax.broadcasted_iota(jnp.int32, (1, slots), 1)
    for x in range(count_x):
        for y in range(count_y):
            for z in range(layers):
                at = slice(z, z + 1)
                for f in range(3):
                    own_ref[x, y, z, f : f + 1, :] = offsets_ref[f, x, y, at, :]
                    own_ref[x, y, z, 3 + f : 4 + f, :] = velocity_ref[f, x, y, at, :]
                own_ref[x, y, z, 6:7, :] = jnp.where(
                    lane < counts_ref[x, y, z], mass_ref[x, y, at, :], 0.0
                )
                own_ref[x, y, z, 7:8, :] = energy_ref[x, y, at, :]
    pl.semaphore_wait(barrier, len(peers))
    copies = start_copies(peers, own_ref, ext_ref, count_x, count_y, send_sem, recv_sem)

    rows = lax.broadcasted_iota(jnp.int32, (8, slots), 0)

    def first_row(x, y, z):
        return ((x * size_y + y) * layers + z) * slots

    def enter(cell, x, y, z):
        shift = jnp.where(
            rows == 0, float(x - 1) - 0.5 * count_x,
            jnp.where(rows == 1, float(y - 1) - 0.5 * count_y, float(z) - 0.5 * layers),
        )
        placed = jnp.where(rows < 3, (cell + shift) * (1.0 / SMOOTHING), cell)
        other = pltpu.roll(placed, 5, 0)
        length = jnp.sum(jnp.where(rows < 3, placed * placed, 0.0), axis=0, keepdims=True)
        moving = jnp.sum(jnp.where(rows < 3, placed * other, 0.0), axis=0, keepdims=True)
        features = jnp.where(rows < 6, placed, jnp.where(rows == 6, length, moving))
        high, middle, low = split(features)
        ones = jnp.where(rows < 3, 1.0, 0.0)
        raw = jnp.where(rows == 3, placed[6:7], placed)
        tile = jnp.concatenate([high, high, high, middle, middle, low, ones, raw], axis=0).T
        at = pl.ds(first_row(x, y, z), slots)
        list_ref[at, 0:DEPTH] = tile
        left_ref[at, 0:DEPTH] = tile.astype(jnp.bfloat16)
        return placed, other, length, moving

    def coefficients(terms, constant):
        high, middle, low = split(terms)
        parts = split(constant)
        last = jnp.where(
            rows == 0, parts[0], jnp.where(rows == 1, parts[1], jnp.where(rows == 2, parts[2], 0.0))
        )
        tile = jnp.concatenate(
            [high, middle, low, high, middle, high, last, jnp.zeros_like(last)], axis=0
        )
        return tile.astype(jnp.bfloat16)

    def products(first, count, column, width):
        return jnp.dot(
            left_ref[pl.ds(pl.multiple_of(first, slots), count), 0:DEPTH],
            right_ref[column, :, 0:width],
            preferred_element_type=jnp.float32,
        )

    def sweep(pairs, count, width, held_ref, process):
        owners = [column for column, _ in pairs]
        blocks = [first // count for _, first in pairs]

        def at(step):
            return look_up(step, owners), look_up(step, blocks) * count

        held_ref[...] = products(pairs[0][1], count, owners[0], width)

        def body(step, carry):
            column, first = at(step)
            next_column, next_first = at(jnp.minimum(step + 1, len(pairs) - 1))
            following = products(next_first, count, next_column, width)
            process(column, pl.multiple_of(first, slots))
            held_ref[...] = following
            return carry

        lax.fori_loop(0, len(pairs), body, 0)

    def density_step(column, first):
        mass = list_ref[pl.ds(first, span), 0:DEPTH][:, RAW + 3 : RAW + 4]
        dist = jnp.maximum(dist_ref[...], TINY)
        q = dist * lax.rsqrt(dist)
        outer = jnp.maximum(2.0 - q, 0.0)
        kernel = jnp.where(q < 1.0, 4.0 - 3.0 * (dist * outer), outer * outer * outer)
        total_ref[column] = total_ref[column] + fold(kernel * mass)

    def force_step(column, first):
        near = list_ref[pl.ds(first, slots), :]
        dist = pair_ref[:, 0:span]
        approach = pair_ref[:, span : 2 * span]
        safe = jnp.maximum(dist, TINY)
        inverse = lax.rsqrt(safe)
        q = safe * inverse
        outer = jnp.maximum(2.0 - q, 0.0)
        slope = jnp.where(q < 1.0, 4.0 - 3.0 * q, outer * outer * inverse)
        mu = jnp.minimum(approach, 0.0) / (dist + SOFTENING)
        sound = mine_ref[column, 1:2, :] + near[:, THERMAL + 1 : THERMAL + 2]
        dense = mine_ref[column, 2:3, :] + near[:, THERMAL + 2 : THERMAL + 3]
        viscous = mu * (mu - sound) / dense
        pressure = mine_ref[column, 0:1, :]
        weight = near[:, RAW + 3 : RAW + 4] * slope
        push = weight * (viscous + (pressure + near[:, THERMAL : THERMAL + 1]))
        heat = weight * (viscous + 2.0 * pressure) * approach
        sums_ref[column, 0] = sums_ref[column, 0] + fold(push)
        for f in range(3):
            sums_ref[column, 1 + f] = sums_ref[column, 1 + f] + fold(push * near[:, RAW + f : RAW + f + 1])
        sums_ref[column, 4] = sums_ref[column, 4] + fold(heat)

    def pairs_of(inside, parts):
        result = []
        for column, (x, y) in enumerate(own):
            for near_x in (x - 1, x, x + 1):
                for near_y in (y - 1, y, y + 1):
                    if ((near_x, near_y) in own) == inside:
                        for z in range(0, layers, layers // parts):
                            result.append((column, first_row(near_x, near_y, z)))
        return result

    for column, (x, y) in enumerate(own):
        for z in range(layers):
            placed, other, length, moving = enter(own_ref[x - 1, y - 1, z], x, y, z)
            lanes = pl.ds(z * slots, slots)
            gap = jnp.where(rows < 3, -2.0 * placed, jnp.where(rows == 6, 1.0, 0.0))
            right_ref[column, :, lanes] = coefficients(gap, length)
            swapped = jnp.where(rows < 3, other, pltpu.roll(placed, 3, 0))
            rate = jnp.where(rows < 6, -swapped, jnp.where(rows == 7, 1.0, 0.0))
            right_ref[column, :, pl.ds(span + z * slots, slots)] = coefficients(rate, moving)
            mine_ref[column, 8:16, lanes] = placed
    total_ref[...] = jnp.zeros_like(total_ref)
    sums_ref[...] = jnp.zeros_like(sums_ref)
    sweep(pairs_of(True, 1), span, span, dist_ref, density_step)
    for copy in copies:
        copy.wait()
    for x in range(count_x + 2):
        for y in range(count_y + 2):
            if (x, y) not in own:
                for z in range(layers):
                    enter(ext_ref[x, y, z], x, y, z)
    sweep(pairs_of(False, 1), span, span, dist_ref, density_step)
    for column, (x, y) in enumerate(own):
        value = jnp.sum(total_ref[column], axis=0, keepdims=True) * (0.25 * NORMALISE)
        for z in range(layers):
            held = own_ref[x - 1, y - 1, z, 6:7, :] > 0.0
            row = value[:, z * slots : (z + 1) * slots]
            safe_ref[x - 1, y - 1, z : z + 1, :] = jnp.where(held, row, 1.0)
            density_out[x - 1, y - 1, z : z + 1, :] = jnp.where(held, row, 0.0)
    copies = start_copies(peers, safe_ref, near_ref, count_x, count_y, rho_send, rho_recv)
    for column, (x, y) in enumerate(own):
        for z in range(layers):
            heat = thermal_rows(own_ref[x - 1, y - 1, z, 7:8, :], safe_ref[x - 1, y - 1, z : z + 1, :])
            mine_ref[column, 0:8, pl.ds(z * slots, slots)] = heat
            list_ref[pl.ds(first_row(x, y, z), slots), THERMAL : THERMAL + 8] = heat.T
    sweep(pairs_of(True, layers), slots, 2 * span, pair_ref, force_step)
    for copy in copies:
        copy.wait()
    for x in range(count_x + 2):
        for y in range(count_y + 2):
            if (x, y) not in own:
                for z in range(layers):
                    heat = thermal_rows(ext_ref[x, y, z, 7:8, :], near_ref[x, y, z : z + 1, :])
                    list_ref[pl.ds(first_row(x, y, z), slots), THERMAL : THERMAL + 8] = heat.T
    sweep(pairs_of(False, layers), slots, 2 * span, pair_ref, force_step)
    factor = 0.75 * NORMALISE / SMOOTHING
    for column, (x, y) in enumerate(own):
        sums = [jnp.sum(sums_ref[column, k], axis=0, keepdims=True) for k in range(SUMS)]
        for z in range(layers):
            held = own_ref[x - 1, y - 1, z, 6:7, :] > 0.0
            lanes = slice(z * slots, (z + 1) * slots)
            for f in range(3):
                value = mine_ref[column, 8 + f : 9 + f, lanes] * sums[0][:, lanes] - sums[1 + f][:, lanes]
                accel_out[f, x - 1, y - 1, z : z + 1, :] = jnp.where(held, value * factor, 0.0)
            heat_out[x - 1, y - 1, z : z + 1, :] = jnp.where(held, sums[4][:, lanes] * (-0.5 * factor), 0.0)


def shards(offsets, velocity, mass, energy, counts):
    slots = mass.shape[-1]
    count_x, count_y, layers = mass.shape[:3]
    wide_x, wide_y = count_x + 2, count_y + 2
    cells = wide_x * wide_y * layers
    own = count_x * count_y
    span = layers * slots
    vmem = pl.BlockSpec(memory_space=VMEM)
    sems = pltpu.SemaphoreType.DMA((len(DIRECTIONS),))
    cell_shape = (layers, 8, slots)
    return pl.pallas_call(
        functools.partial(sph_kernel, lax.axis_size("gx"), lax.axis_size("gy")),
        out_shape=[
            jax.ShapeDtypeStruct(mass.shape, jnp.float32),
            jax.ShapeDtypeStruct((3,) + mass.shape, jnp.float32),
            jax.ShapeDtypeStruct(mass.shape, jnp.float32),
        ],
        in_specs=[pl.BlockSpec(memory_space=pl.ANY)] * 4 + [pl.BlockSpec(memory_space=pltpu.SMEM)],
        out_specs=[vmem, vmem, vmem],
        scratch_shapes=[
            VMEM(offsets.shape, jnp.float32),
            VMEM(velocity.shape, jnp.float32),
            VMEM(mass.shape, jnp.float32),
            VMEM(energy.shape, jnp.float32),
            VMEM((count_x, count_y) + cell_shape, jnp.float32),
            VMEM((wide_x, wide_y) + cell_shape, jnp.float32),
            VMEM((count_x, count_y, layers, slots), jnp.float32),
            VMEM((wide_x, wide_y, layers, slots), jnp.float32),
            VMEM((cells * slots, 128), jnp.float32),
            VMEM((cells * slots, 128), jnp.bfloat16),
            VMEM((own, DEPTH, 2 * span), jnp.bfloat16),
            VMEM((own, 16, span), jnp.float32),
            VMEM((own, 8, span), jnp.float32),
            VMEM((own, SUMS, 8, span), jnp.float32),
            VMEM((span, span), jnp.float32),
            VMEM((slots, 2 * span), jnp.float32),
            sems,
            sems,
            sems,
            sems,
            pltpu.SemaphoreType.DMA((4,)),
        ],
        compiler_params=pltpu.CompilerParams(collective_id=0, has_side_effects=True),
        name="sph",
    )(offsets, velocity, mass, energy, counts)


def solution(mesh):
    in_specs = (
        P(None, "gx", "gy", None, None),
        P(None, "gx", "gy", None, None),
        P("gx", "gy", None, None),
        P("gx", "gy", None, None),
        P("gx", "gy", None),
    )
    out_specs = (
        P("gx", "gy", None, None),
        P(None, "gx", "gy", None, None),
        P("gx", "gy", None, None),
    )
    return jax.shard_map(shards, mesh=mesh, in_specs=in_specs, out_specs=out_specs, check_vma=False)
```

```python
import functools
import math

import jax
import jax.numpy as jnp
from jax import lax
from jax.experimental import pallas as pl
from jax.experimental.pallas import tpu as pltpu
from jax.sharding import PartitionSpec as P

SMOOTHING = 0.5
NORMALISE = 1.0 / (math.pi * 0.125)
ADIABATIC = 5.0 / 3.0
VISC_ALPHA = 1.0
VISC_BETA = 2.0
SOFTENING = 0.01
TINY = 1e-30
VMEM = pltpu.VMEM
MESH = pl.DeviceIdType.MESH
DIRECTIONS = [(dx, dy) for dx in (-1, 0, 1) for dy in (-1, 0, 1) if (dx, dy) != (0, 0)]
RAW = 56
DEPTH = 64
DEEP = 96
SUMS = 5
TERMS = 5


def edge(step, count):
    if step == 0:
        return (0, 1, count)
    if step == 1:
        return (count - 1, 0, 1)
    return (0, count + 1, 1)


def start_copies(peers, own_ref, out_ref, count_x, count_y, send_sem, recv_sem):
    copies = []
    for k, (dx, dy) in enumerate(DIRECTIONS):
        from_x, to_x, width_x = edge(dx, count_x)
        from_y, to_y, width_y = edge(dy, count_y)
        copy = pltpu.make_async_remote_copy(
            src_ref=own_ref.at[pl.ds(from_x, width_x), pl.ds(from_y, width_y)],
            dst_ref=out_ref.at[pl.ds(to_x, width_x), pl.ds(to_y, width_y)],
            send_sem=send_sem.at[k],
            recv_sem=recv_sem.at[k],
            device_id=peers[k],
            device_id_type=MESH,
        )
        copy.start()
        copies.append(copy)
    return copies


def split(values):
    high = values.astype(jnp.bfloat16).astype(jnp.float32)
    rest = values - high
    middle = rest.astype(jnp.bfloat16).astype(jnp.float32)
    return high, middle, rest - middle


def look_up(step, values):
    result = step + values[0]
    for k in range(1, len(values)):
        jump = values[k] - values[k - 1] - 1
        if jump:
            result = result + jnp.where(step >= k, jump, 0)
    return result


def fold(values):
    return jnp.sum(values.reshape(values.shape[0] // 8, 8, values.shape[1]), axis=0)


def thermal_rows(energy, rho):
    pressure = (ADIABATIC - 1.0) * energy / rho
    sound = jnp.sqrt(ADIABATIC * (ADIABATIC - 1.0) * energy) * (0.5 * VISC_ALPHA / VISC_BETA)
    dense = rho * (0.5 / VISC_BETA)
    rows = lax.broadcasted_iota(jnp.int32, (8, energy.shape[1]), 0)
    return jnp.where(rows == 0, pressure, jnp.where(rows == 1, sound, jnp.where(rows == 2, dense, 0.0)))


def sph_kernel(
    size_gx, size_gy, offsets_hbm, velocity_hbm, mass_hbm, energy_hbm, counts_ref,
    density_out, accel_out, heat_out,
    offsets_ref, velocity_ref, mass_ref, energy_ref, own_ref, ext_ref, safe_ref, near_ref,
    list_ref, left_ref, right_ref, mine_ref, total_ref, sums_ref, dist_ref, pair_ref,
    send_sem, recv_sem, rho_send, rho_recv, in_sem,
):
    count_x, count_y, layers, _, slots = own_ref.shape
    size_y = count_y + 2
    span = layers * slots
    own = [(x, y) for x in range(1, count_x + 1) for y in range(1, count_y + 1)]
    my_x, my_y = lax.axis_index("gx"), lax.axis_index("gy")
    barrier = pltpu.get_barrier_semaphore()
    peers = []
    for dx, dy in DIRECTIONS:
        peers.append(
            (lax.rem(my_x + dx + size_gx, size_gx), lax.rem(my_y + dy + size_gy, size_gy))
        )
    for peer in peers:
        pl.semaphore_signal(barrier, inc=1, device_id=peer, device_id_type=MESH)
    sources = (offsets_hbm, velocity_hbm, mass_hbm, energy_hbm)
    targets = (offsets_ref, velocity_ref, mass_ref, energy_ref)
    loads = [pltpu.make_async_copy(a, b, in_sem.at[k]) for k, (a, b) in enumerate(zip(sources, targets))]
    for load in loads:
        load.start()
    for load in loads:
        load.wait()
    lane = lax.broadcasted_iota(jnp.int32, (1, slots), 1)
    for x in range(count_x):
        for y in range(count_y):
            for z in range(layers):
                at = slice(z, z + 1)
                for f in range(3):
                    own_ref[x, y, z, f : f + 1, :] = offsets_ref[f, x, y, at, :]
                    own_ref[x, y, z, 3 + f : 4 + f, :] = velocity_ref[f, x, y, at, :]
                own_ref[x, y, z, 6:7, :] = jnp.where(
                    lane < counts_ref[x, y, z], mass_ref[x, y, at, :], 0.0
                )
                own_ref[x, y, z, 7:8, :] = energy_ref[x, y, at, :]
    pl.semaphore_wait(barrier, len(peers))
    copies = start_copies(peers, own_ref, ext_ref, count_x, count_y, send_sem, recv_sem)

    rows = lax.broadcasted_iota(jnp.int32, (8, slots), 0)

    def first_row(x, y, z):
        return ((x * size_y + y) * layers + z) * slots

    def enter(cell, x, y, z):
        shift = jnp.where(
            rows == 0, float(x - 1) - 0.5 * count_x,
            jnp.where(rows == 1, float(y - 1) - 0.5 * count_y, float(z) - 0.5 * layers),
        )
        placed = jnp.where(rows < 3, (cell + shift) * (1.0 / SMOOTHING), cell)
        other = pltpu.roll(placed, 5, 0)
        length = jnp.sum(jnp.where(rows < 3, placed * placed, 0.0), axis=0, keepdims=True)
        moving = jnp.sum(jnp.where(rows < 3, placed * other, 0.0), axis=0, keepdims=True)
        features = jnp.where(rows < 6, placed, jnp.where(rows == 6, length, moving))
        high, middle, low = split(features)
        ones = jnp.where(rows < 3, 1.0, 0.0)
        raw = jnp.where(rows == 3, placed[6:7], placed)
        tile = jnp.concatenate([high, high, high, middle, middle, low, ones, raw], axis=0).T
        at = pl.ds(first_row(x, y, z), slots)
        list_ref[at, 0:DEPTH] = tile
        left_ref[at, 0:DEPTH] = tile.astype(jnp.bfloat16)
        return placed, other, length, moving

    def coefficients(terms, constant):
        high, middle, low = split(terms)
        none = jnp.zeros_like(terms)
        parts = [high, middle, low, high, middle, high, constant_rows(constant)] + [none] * 5
        return jnp.concatenate(parts, axis=0).astype(jnp.bfloat16)

    def constant_rows(constant):
        parts = split(constant)
        return jnp.where(
            rows == 0, parts[0], jnp.where(rows == 1, parts[1], jnp.where(rows == 2, parts[2], 0.0))
        )

    def enter_thermal(energy, rho, x, y, z):
        thermal = thermal_rows(energy, rho)
        parts = list(split(thermal)) + [jnp.zeros_like(thermal)] * 5
        tile = jnp.concatenate(parts, axis=0).T
        left_ref[pl.ds(first_row(x, y, z), slots), DEPTH:DEEP] = tile[:, 0 : DEEP - DEPTH].astype(jnp.bfloat16)
        return thermal

    def products(first, count, column, depth, width):
        return jnp.dot(
            left_ref[pl.ds(pl.multiple_of(first, slots), count), 0:depth],
            right_ref[column, 0:depth, 0:width],
            preferred_element_type=jnp.float32,
        )

    def sweep(pairs, count, depth, width, held_ref, process):
        owners = [column for column, _ in pairs]
        blocks = [first // count for _, first in pairs]

        def at(step):
            return look_up(step, owners), look_up(step, blocks) * count

        held_ref[...] = products(pairs[0][1], count, owners[0], depth, width)

        def body(step, carry):
            column, first, next_column, next_first = carry
            following = products(next_first, count, next_column, depth, width)
            process(column, pl.multiple_of(first, slots))
            held_ref[...] = following
            return (next_column, next_first) + at(jnp.minimum(step + 2, len(pairs) - 1))

        start = tuple(jnp.int32(value) for value in pairs[0] + pairs[min(1, len(pairs) - 1)])
        lax.fori_loop(0, len(pairs), body, start)

    def density_step(column, first):
        mass = list_ref[pl.ds(first, span), 0:DEPTH][:, RAW + 3 : RAW + 4]
        dist = jnp.maximum(dist_ref[...], TINY)
        q = dist * lax.rsqrt(dist)
        outer = jnp.maximum(2.0 - q, 0.0)
        kernel = jnp.where(q < 1.0, 4.0 - 3.0 * (dist * outer), outer * outer * outer)
        total_ref[column] = total_ref[column] + fold(kernel * mass)

    def force_step(column, first):
        near = list_ref[pl.ds(first, slots), 0:DEPTH]
        dist, approach, sound, dense, pressure = (
            pair_ref[:, k * span : (k + 1) * span] for k in range(TERMS)
        )
        safe = jnp.maximum(dist, TINY)
        inverse = lax.rsqrt(safe)
        q = safe * inverse
        outer = jnp.maximum(2.0 - q, 0.0)
        slope = jnp.where(q < 1.0, 4.0 - 3.0 * q, outer * outer * inverse)
        mu = jnp.minimum(approach, 0.0) / (dist + SOFTENING)
        viscous = mu * (mu - sound) / dense
        weight = near[:, RAW + 3 : RAW + 4] * slope
        push = weight * (viscous + pressure)
        heat = weight * (viscous + mine_ref[column, 3:4, :]) * approach
        sums_ref[column, 0] = sums_ref[column, 0] + fold(push)
        for f in range(3):
            sums_ref[column, 1 + f] = sums_ref[column, 1 + f] + fold(push * near[:, RAW + f : RAW + f + 1])
        sums_ref[column, 4] = sums_ref[column, 4] + fold(heat)

    def pairs_of(inside, parts):
        result = []
        for column, (x, y) in enumerate(own):
            for near_x in (x - 1, x, x + 1):
                for near_y in (y - 1, y, y + 1):
                    if ((near_x, near_y) in own) == inside:
                        for z in range(0, layers, layers // parts):
                            result.append((column, first_row(near_x, near_y, z)))
        return result

    for column, (x, y) in enumerate(own):
        for z in range(layers):
            placed, other, length, moving = enter(own_ref[x - 1, y - 1, z], x, y, z)
            lanes = pl.ds(z * slots, slots)
            gap = jnp.where(rows < 3, -2.0 * placed, jnp.where(rows == 6, 1.0, 0.0))
            right_ref[column, :, lanes] = coefficients(gap, length)
            swapped = jnp.where(rows < 3, other, pltpu.roll(placed, 3, 0))
            rate = jnp.where(rows < 6, -swapped, jnp.where(rows == 7, 1.0, 0.0))
            right_ref[column, :, pl.ds(span + z * slots, slots)] = coefficients(rate, moving)
            mine_ref[column, 8:16, lanes] = placed
    total_ref[...] = jnp.zeros_like(total_ref)
    sums_ref[...] = jnp.zeros_like(sums_ref)
    sweep(pairs_of(True, 1), span, DEPTH, span, dist_ref, density_step)
    for copy in copies:
        copy.wait()
    for x in range(count_x + 2):
        for y in range(count_y + 2):
            if (x, y) not in own:
                for z in range(layers):
                    enter(ext_ref[x, y, z], x, y, z)
    sweep(pairs_of(False, 1), span, DEPTH, span, dist_ref, density_step)
    for column, (x, y) in enumerate(own):
        value = jnp.sum(total_ref[column], axis=0, keepdims=True) * (0.25 * NORMALISE)
        for z in range(layers):
            held = own_ref[x - 1, y - 1, z, 6:7, :] > 0.0
            row = value[:, z * slots : (z + 1) * slots]
            safe_ref[x - 1, y - 1, z : z + 1, :] = jnp.where(held, row, 1.0)
            density_out[x - 1, y - 1, z : z + 1, :] = jnp.where(held, row, 0.0)
    copies = start_copies(peers, safe_ref, near_ref, count_x, count_y, rho_send, rho_recv)
    for column, (x, y) in enumerate(own):
        for z in range(layers):
            energy, rho = own_ref[x - 1, y - 1, z, 7:8, :], safe_ref[x - 1, y - 1, z : z + 1, :]
            thermal = enter_thermal(energy, rho, x, y, z)
            mine_ref[column, 3:4, pl.ds(z * slots, slots)] = 2.0 * thermal[0:1]
            none = jnp.zeros_like(thermal)
            for k, row in enumerate((1, 2, 0)):
                one = jnp.where(rows == row, 1.0, 0.0)
                parts = [none] * 6 + [constant_rows(thermal[row : row + 1]), none, one, one, one, none]
                lanes = pl.ds((2 + k) * span + z * slots, slots)
                right_ref[column, :, lanes] = jnp.concatenate(parts, axis=0).astype(jnp.bfloat16)
    sweep(pairs_of(True, layers), slots, DEEP, TERMS * span, pair_ref, force_step)
    for copy in copies:
        copy.wait()
    for x in range(count_x + 2):
        for y in range(count_y + 2):
            if (x, y) not in own:
                for z in range(layers):
                    enter_thermal(ext_ref[x, y, z, 7:8, :], near_ref[x, y, z : z + 1, :], x, y, z)
    sweep(pairs_of(False, layers), slots, DEEP, TERMS * span, pair_ref, force_step)
    factor = 0.75 * NORMALISE / SMOOTHING
    for column, (x, y) in enumerate(own):
        sums = [jnp.sum(sums_ref[column, k], axis=0, keepdims=True) for k in range(SUMS)]
        for z in range(layers):
            held = own_ref[x - 1, y - 1, z, 6:7, :] > 0.0
            lanes = slice(z * slots, (z + 1) * slots)
            for f in range(3):
                value = mine_ref[column, 8 + f : 9 + f, lanes] * sums[0][:, lanes] - sums[1 + f][:, lanes]
                accel_out[f, x - 1, y - 1, z : z + 1, :] = jnp.where(held, value * factor, 0.0)
            heat_out[x - 1, y - 1, z : z + 1, :] = jnp.where(held, sums[4][:, lanes] * (-0.5 * factor), 0.0)


def finish_kernel(density_ref, accel_ref, heat_ref, density_out, accel_out, heat_out):
    density_out[...] = density_ref[...]
    accel_out[...] = accel_ref[...]
    heat_out[...] = heat_ref[...]


def shards(offsets, velocity, mass, energy, counts):
    slots = mass.shape[-1]
    count_x, count_y, layers = mass.shape[:3]
    wide_x, wide_y = count_x + 2, count_y + 2
    cells = wide_x * wide_y * layers
    own = count_x * count_y
    span = layers * slots
    vmem = pl.BlockSpec(memory_space=VMEM)
    shapes = (mass.shape, (3,) + mass.shape, mass.shape)
    sems = pltpu.SemaphoreType.DMA((len(DIRECTIONS),))
    cell_shape = (layers, 8, slots)
    results = pl.pallas_call(
        functools.partial(sph_kernel, lax.axis_size("gx"), lax.axis_size("gy")),
        out_shape=[VMEM(shape, jnp.float32) for shape in shapes],
        in_specs=[pl.BlockSpec(memory_space=pl.ANY)] * 4 + [pl.BlockSpec(memory_space=pltpu.SMEM)],
        out_specs=[vmem, vmem, vmem],
        scratch_shapes=[
            VMEM(offsets.shape, jnp.float32),
            VMEM(velocity.shape, jnp.float32),
            VMEM(mass.shape, jnp.float32),
            VMEM(energy.shape, jnp.float32),
            VMEM((count_x, count_y) + cell_shape, jnp.float32),
            VMEM((wide_x, wide_y) + cell_shape, jnp.float32),
            VMEM((count_x, count_y, layers, slots), jnp.float32),
            VMEM((wide_x, wide_y, layers, slots), jnp.float32),
            VMEM((cells * slots, 128), jnp.float32),
            VMEM((cells * slots, 128), jnp.bfloat16),
            VMEM((own, DEEP, TERMS * span), jnp.bfloat16),
            VMEM((own, 16, span), jnp.float32),
            VMEM((own, 8, span), jnp.float32),
            VMEM((own, SUMS, 8, span), jnp.float32),
            VMEM((span, span), jnp.float32),
            VMEM((slots, TERMS * span), jnp.float32),
            sems,
            sems,
            sems,
            sems,
            pltpu.SemaphoreType.DMA((4,)),
        ],
        compiler_params=pltpu.CompilerParams(collective_id=0, has_side_effects=True),
        name="sph",
    )(offsets, velocity, mass, energy, counts)
    return pl.pallas_call(
        finish_kernel,
        out_shape=[jax.ShapeDtypeStruct(shape, jnp.float32) for shape in shapes],
        in_specs=[vmem] * 3,
        out_specs=[vmem] * 3,
        name="finish",
    )(*[pltpu.with_memory_space_constraint(result, VMEM) for result in results])


def solution(mesh):
    in_specs = (
        P(None, "gx", "gy", None, None),
        P(None, "gx", "gy", None, None),
        P("gx", "gy", None, None),
        P("gx", "gy", None, None),
        P("gx", "gy", None),
    )
    out_specs = (
        P("gx", "gy", None, None),
        P(None, "gx", "gy", None, None),
        P("gx", "gy", None, None),
    )
    return jax.shard_map(shards, mesh=mesh, in_specs=in_specs, out_specs=out_specs, check_vma=False)
```

```python
import functools
import math

import jax
import jax.numpy as jnp
from jax import lax
from jax.experimental import pallas as pl
from jax.experimental.pallas import tpu as pltpu
from jax.sharding import PartitionSpec as P

SMOOTHING = 0.5
NORMALISE = 1.0 / (math.pi * 0.125)
ADIABATIC = 5.0 / 3.0
VISC_ALPHA = 1.0
VISC_BETA = 2.0
SOFTENING = 0.01
TINY = 1e-30
VMEM = pltpu.VMEM
MESH = pl.DeviceIdType.MESH
DIRECTIONS = [(dx, dy) for dx in (-1, 0, 1) for dy in (-1, 0, 1) if (dx, dy) != (0, 0)]
DEPTH = 64
SUMS = 5
CHUNK = 64


def edge(step, count):
    if step == 0:
        return (0, 1, count)
    if step == 1:
        return (count - 1, 0, 1)
    return (0, count + 1, 1)


def start_copies(peers, own_ref, out_ref, count_x, count_y, send_sem, recv_sem):
    copies = []
    for k, (dx, dy) in enumerate(DIRECTIONS):
        from_x, to_x, width_x = edge(dx, count_x)
        from_y, to_y, width_y = edge(dy, count_y)
        copy = pltpu.make_async_remote_copy(
            src_ref=own_ref.at[pl.ds(from_x, width_x), pl.ds(from_y, width_y)],
            dst_ref=out_ref.at[pl.ds(to_x, width_x), pl.ds(to_y, width_y)],
            send_sem=send_sem.at[k],
            recv_sem=recv_sem.at[k],
            device_id=peers[k],
            device_id_type=MESH,
        )
        copy.start()
        copies.append(copy)
    return copies


def split(values):
    high = values.astype(jnp.bfloat16).astype(jnp.float32)
    rest = values - high
    middle = rest.astype(jnp.bfloat16).astype(jnp.float32)
    return high, middle, rest - middle


def look_up(step, values):
    result = step + values[0]
    for k in range(1, len(values)):
        jump = values[k] - values[k - 1] - 1
        if jump:
            result = result + jnp.where(step >= k, jump, 0)
    return result


def fold(values, slots):
    total = values[:, 0:slots]
    for k in range(slots, values.shape[1], slots):
        total = total + values[:, k : k + slots]
    return total


def thermal_rows(energy, rho):
    pressure = (ADIABATIC - 1.0) * energy / rho
    sound = jnp.sqrt(ADIABATIC * (ADIABATIC - 1.0) * energy) * (0.5 * VISC_ALPHA / VISC_BETA)
    dense = rho * (0.5 / VISC_BETA)
    rows = lax.broadcasted_iota(jnp.int32, (8, energy.shape[1]), 0)
    return jnp.where(rows == 0, pressure, jnp.where(rows == 1, sound, jnp.where(rows == 2, dense, 0.0)))


def sph_kernel(
    size_gx, size_gy, offsets_hbm, velocity_hbm, mass_hbm, energy_hbm, counts_ref,
    density_out, accel_out, heat_out,
    offsets_ref, velocity_ref, mass_ref, energy_ref, own_ref, ext_ref, safe_ref, near_ref,
    left_ref, right_ref, near_row_ref, warm_row_ref, mine_ref, total_ref, sums_ref, dist_ref, pair_ref,
    send_sem, recv_sem, rho_send, rho_recv, in_sem,
):
    count_x, count_y, layers, _, slots = own_ref.shape
    size_y = count_y + 2
    span = layers * slots
    own = [(x, y) for x in range(1, count_x + 1) for y in range(1, count_y + 1)]
    my_x, my_y = lax.axis_index("gx"), lax.axis_index("gy")
    barrier = pltpu.get_barrier_semaphore()
    peers = []
    for dx, dy in DIRECTIONS:
        peers.append(
            (lax.rem(my_x + dx + size_gx, size_gx), lax.rem(my_y + dy + size_gy, size_gy))
        )
    for peer in peers:
        pl.semaphore_signal(barrier, inc=1, device_id=peer, device_id_type=MESH)
    sources = (offsets_hbm, velocity_hbm, mass_hbm, energy_hbm)
    targets = (offsets_ref, velocity_ref, mass_ref, energy_ref)
    loads = [pltpu.make_async_copy(a, b, in_sem.at[k]) for k, (a, b) in enumerate(zip(sources, targets))]
    for load in loads:
        load.start()
    for load in loads:
        load.wait()
    lane = lax.broadcasted_iota(jnp.int32, (1, slots), 1)
    for x in range(count_x):
        for y in range(count_y):
            for z in range(layers):
                at = slice(z, z + 1)
                for f in range(3):
                    own_ref[x, y, z, f : f + 1, :] = offsets_ref[f, x, y, at, :]
                    own_ref[x, y, z, 3 + f : 4 + f, :] = velocity_ref[f, x, y, at, :]
                own_ref[x, y, z, 6:7, :] = jnp.where(
                    lane < counts_ref[x, y, z], mass_ref[x, y, at, :], 0.0
                )
                own_ref[x, y, z, 7:8, :] = energy_ref[x, y, at, :]
    rows = lax.broadcasted_iota(jnp.int32, (8, slots), 0)
    none = jnp.zeros((8, slots), jnp.float32)
    inner_x, inner_y = range(1, count_x + 1), range(1, count_y + 1)
    low_first = my_y > 0
    side = jnp.where(low_first, 0, count_y + 1)
    other_side = jnp.where(low_first, count_y + 1, 0)

    def place(cell, x, y, z):
        middle_y = jnp.asarray(y, jnp.float32) - (1.0 + 0.5 * count_y)
        shift = jnp.where(
            rows == 0, float(x - 1) - 0.5 * count_x, jnp.where(rows == 1, middle_y, float(z) - 0.5 * layers)
        )
        placed = jnp.where(rows < 3, (cell + shift) * (1.0 / SMOOTHING), cell)
        other = pltpu.roll(placed, 5, 0)
        length = jnp.sum(jnp.where(rows < 3, placed * placed, 0.0), axis=0, keepdims=True)
        moving = jnp.sum(jnp.where(rows < 3, placed * other, 0.0), axis=0, keepdims=True)
        return placed, other, length, moving

    def enter(placed, length, moving, x, y, z):
        block, lanes = x * size_y + y, pl.ds(z * slots, slots)
        features = jnp.where(rows < 6, placed, jnp.where(rows == 6, length, moving))
        high, middle, low = split(features)
        ones = jnp.where(rows < 3, 1.0, 0.0)
        tile = jnp.concatenate([high, high, high, middle, middle, low, ones, none], axis=0)
        right_ref[block, :, lanes] = tile.astype(jnp.bfloat16)
        near_row_ref[block, :, lanes] = placed

    def enter_near(x, y, z):
        placed, _, length, moving = place(ext_ref[x, y, z], x, y, z)
        enter(placed, length, moving, x, y, z)

    def coefficients(terms, constant):
        high, middle, low = split(terms)
        parts = split(constant)
        last = jnp.where(
            rows == 0, parts[0], jnp.where(rows == 1, parts[1], jnp.where(rows == 2, parts[2], 0.0))
        )
        tile = jnp.concatenate([high, middle, low, high, middle, high, last, none], axis=0)
        return tile.T.astype(jnp.bfloat16)

    def products(column, block, count):
        return jnp.dot(
            left_ref[column, 0:count, 0:DEPTH], right_ref[block], preferred_element_type=jnp.float32
        )

    def sweep(pairs, count, held_ref, process):
        tables = pairs if isinstance(pairs, tuple) else (pairs,)
        length = len(tables[0])

        def at(step):
            found = [tuple(look_up(step, [pair[k] for pair in table]) for k in range(2)) for table in tables]
            if len(found) == 1:
                return found[0]
            return tuple(jnp.where(low_first, a, b) for a, b in zip(*found))

        def step_zero(step):
            found = [table[min(step, length - 1)] for table in tables]
            if len(found) == 1:
                return tuple(jnp.int32(value) for value in found[0])
            return tuple(jnp.where(low_first, a, b) for a, b in zip(*found))

        start = step_zero(0) + step_zero(1)
        held_ref[...] = products(start[0], start[1], count)

        def body(step, carry):
            column, block, next_column, next_block = carry
            following = products(next_column, next_block, count)
            process(column, block)
            held_ref[...] = following
            return (next_column, next_block) + at(jnp.minimum(step + 2, length - 1))

        lax.fori_loop(0, length, body, start, unroll=2)

    def density_step(column, block):
        mass = near_row_ref[block, 6:7, :]
        for first in range(0, span, CHUNK):
            at = slice(first, first + CHUNK)
            dist = jnp.maximum(dist_ref[at, :], TINY)
            outer = jnp.maximum(1.0 - dist * lax.rsqrt(dist), 0.0)
            kernel = jnp.where(dist < 0.25, 0.5 - 3.0 * (dist * outer), outer * outer * outer)
            total_ref[column, at, :] = total_ref[column, at, :] + fold(kernel * mass, slots)

    def force_step(column, block):
        mass = near_row_ref[block, 6:7, :]
        spots = [near_row_ref[block, f : f + 1, :] for f in range(3)]
        near_pressure, near_sound, near_dense = (warm_row_ref[block, k : k + 1, :] for k in range(3))
        for first in range(0, span, CHUNK):
            at = slice(first, first + CHUNK)
            dist, approach = pair_ref[at, :], pair_ref[span + first : span + first + CHUNK, :]
            pressure, sound, dense = (
                jnp.concatenate([mine_ref[column, k, at, :]] * layers, axis=1) for k in range(3)
            )
            safe = jnp.minimum(jnp.maximum(dist, TINY), 1.0)
            inverse = lax.rsqrt(safe)
            half = safe * inverse
            slope = jnp.minimum(inverse, 2.0) + jnp.maximum(half - 2.0, -3.0 * half)
            mu = jnp.minimum(approach, 0.0) / (dist + 0.25 * SOFTENING)
            own_push = mu * (mu - (sound + near_sound)) / (dense + near_dense) + pressure
            weight = mass * slope
            push = weight * (own_push + near_pressure)
            heat = weight * (own_push + pressure) * approach
            terms = [push] + [push * spot for spot in spots] + [heat]
            for k, term in enumerate(terms):
                sums_ref[column, k, at, :] = sums_ref[column, k, at, :] + fold(term, slots)

    def block_of(x, y):
        return x * size_y + y

    def pairs_with(columns):
        result = []
        for near_x, near_y in columns:
            for column, (x, y) in enumerate(own):
                if abs(near_x - x) <= 1 and abs(near_y - y) <= 1:
                    result.append((column, block_of(near_x, near_y)))
        return sorted(result)

    across = [(x, y) for x in (0, count_x + 1) for y in inner_y]
    low_side = [(x, 0) for x in range(count_x + 2)]
    high_side = [(x, count_y + 1) for x in range(count_x + 2)]

    def wait_side(which, copies):
        for copy, (_, dy) in zip(copies, DIRECTIONS):
            if dy == which:
                copy.wait_recv()

    def start_own():
        for column, (x, y) in enumerate(own):
            for z in range(layers):
                placed, other, length, moving = place(own_ref[x - 1, y - 1, z], x, y, z)
                enter(placed, length, moving, x, y, z)
                gap = jnp.where(rows < 3, -0.5 * placed, jnp.where(rows == 6, 0.25, 0.0))
                left_ref[column, pl.ds(z * slots, slots), 0:DEPTH] = coefficients(gap, 0.25 * length)
                swapped = jnp.where(rows < 3, other, pltpu.roll(placed, 3, 0))
                rate = jnp.where(rows < 6, -0.25 * swapped, jnp.where(rows == 7, 0.25, 0.0))
                left_ref[column, pl.ds(span + z * slots, slots), 0:DEPTH] = coefficients(rate, 0.25 * moving)
        total_ref[...] = jnp.zeros_like(total_ref)
        sums_ref[...] = jnp.zeros_like(sums_ref)
        sweep(pairs_with(own), span, dist_ref, density_step)

    first_rows = my_y < 2
    pl.when(first_rows)(start_own)
    pl.semaphore_wait(barrier, len(peers))
    copies = start_copies(peers, own_ref, ext_ref, count_x, count_y, send_sem, recv_sem)
    pl.when(jnp.logical_not(first_rows))(start_own)

    wait_side(0, copies)
    pl.when(low_first)(lambda: wait_side(1, copies))
    pl.when(jnp.logical_not(low_first))(lambda: wait_side(-1, copies))
    for x, y in across:
        for z in range(layers):
            enter_near(x, y, z)
    for x in range(count_x + 2):
        for z in range(layers):
            enter_near(x, side, z)
    sweep(
        (pairs_with(across) + pairs_with(low_side), pairs_with(across) + pairs_with(high_side)),
        span, dist_ref, density_step,
    )
    pl.when(low_first)(lambda: wait_side(-1, copies))
    pl.when(jnp.logical_not(low_first))(lambda: wait_side(1, copies))
    for x in range(count_x + 2):
        for z in range(layers):
            enter_near(x, other_side, z)
    sweep((pairs_with(high_side), pairs_with(low_side)), span, dist_ref, density_step)
    for column, (x, y) in enumerate(own):
        for z in range(layers):
            total = total_ref[column, z * slots : (z + 1) * slots, :].T
            row = jnp.sum(total, axis=0, keepdims=True) * (2.0 * NORMALISE)
            held = own_ref[x - 1, y - 1, z, 6:7, :] > 0.0
            safe_ref[x - 1, y - 1, z : z + 1, :] = jnp.where(held, row, 1.0)
            density_out[x - 1, y - 1, z : z + 1, :] = jnp.where(held, row, 0.0)
    rho_copies = start_copies(peers, safe_ref, near_ref, count_x, count_y, rho_send, rho_recv)
    for copy in copies:
        copy.wait_send()
    for column, (x, y) in enumerate(own):
        for z in range(layers):
            warm = thermal_rows(own_ref[x - 1, y - 1, z, 7:8, :], safe_ref[x - 1, y - 1, z : z + 1, :])
            warm_row_ref[block_of(x, y), :, pl.ds(z * slots, slots)] = warm
            turned = jnp.concatenate([warm] + [none] * 7, axis=0).T
            for k in range(3):
                mine_ref[column, k, pl.ds(z * slots, slots), :] = jnp.broadcast_to(
                    turned[:, k : k + 1], (slots, slots)
                )
    sweep(pairs_with(own), 2 * span, pair_ref, force_step)
    for copy in rho_copies:
        copy.wait()
    halo = across + low_side + high_side
    for x, y in halo:
        for z in range(layers):
            warm = thermal_rows(ext_ref[x, y, z, 7:8, :], near_ref[x, y, z : z + 1, :])
            warm_row_ref[block_of(x, y), :, pl.ds(z * slots, slots)] = warm
    sweep(pairs_with(halo), 2 * span, pair_ref, force_step)
    factor = 1.5 * NORMALISE / SMOOTHING
    for column, (x, y) in enumerate(own):
        for z in range(layers):
            held = own_ref[x - 1, y - 1, z, 6:7, :] > 0.0
            lanes = slice(z * slots, (z + 1) * slots)
            sums = [jnp.sum(sums_ref[column, k, lanes, :].T, axis=0, keepdims=True) for k in range(SUMS)]
            for f in range(3):
                value = near_row_ref[block_of(x, y), f : f + 1, lanes] * sums[0] - sums[1 + f]
                accel_out[f, x - 1, y - 1, z : z + 1, :] = jnp.where(held, value * factor, 0.0)
            heat_out[x - 1, y - 1, z : z + 1, :] = jnp.where(held, sums[4] * (-2.0 * factor), 0.0)


def finish_kernel(density_ref, accel_ref, heat_ref, density_out, accel_out, heat_out):
    density_out[...] = density_ref[...]
    accel_out[...] = accel_ref[...]
    heat_out[...] = heat_ref[...]


def shards(offsets, velocity, mass, energy, counts):
    slots = mass.shape[-1]
    count_x, count_y, layers = mass.shape[:3]
    wide_x, wide_y = count_x + 2, count_y + 2
    own = count_x * count_y
    span = layers * slots
    vmem = pl.BlockSpec(memory_space=VMEM)
    shapes = (mass.shape, (3,) + mass.shape, mass.shape)
    sems = pltpu.SemaphoreType.DMA((len(DIRECTIONS),))
    cell_shape = (layers, 8, slots)
    results = pl.pallas_call(
        functools.partial(sph_kernel, lax.axis_size("gx"), lax.axis_size("gy")),
        out_shape=[VMEM(shape, jnp.float32) for shape in shapes],
        in_specs=[pl.BlockSpec(memory_space=pl.ANY)] * 4 + [pl.BlockSpec(memory_space=pltpu.SMEM)],
        out_specs=[vmem, vmem, vmem],
        scratch_shapes=[
            VMEM(offsets.shape, jnp.float32),
            VMEM(velocity.shape, jnp.float32),
            VMEM(mass.shape, jnp.float32),
            VMEM(energy.shape, jnp.float32),
            VMEM((count_x, count_y) + cell_shape, jnp.float32),
            VMEM((wide_x, wide_y) + cell_shape, jnp.float32),
            VMEM((count_x, count_y, layers, slots), jnp.float32),
            VMEM((wide_x, wide_y, layers, slots), jnp.float32),
            VMEM((own, 2 * span, 128), jnp.bfloat16),
            VMEM((wide_x * wide_y, DEPTH, span), jnp.bfloat16),
            VMEM((wide_x * wide_y, 8, span), jnp.float32),
            VMEM((wide_x * wide_y, 8, span), jnp.float32),
            VMEM((own, 3, span, slots), jnp.float32),
            VMEM((own, span, slots), jnp.float32),
            VMEM((own, SUMS, span, slots), jnp.float32),
            VMEM((span, span), jnp.float32),
            VMEM((2 * span, span), jnp.float32),
            sems,
            sems,
            sems,
            sems,
            pltpu.SemaphoreType.DMA((4,)),
        ],
        compiler_params=pltpu.CompilerParams(collective_id=0, has_side_effects=True),
        name="sph",
    )(offsets, velocity, mass, energy, counts)
    return pl.pallas_call(
        finish_kernel,
        out_shape=[jax.ShapeDtypeStruct(shape, jnp.float32) for shape in shapes],
        in_specs=[vmem] * 3,
        out_specs=[vmem] * 3,
        name="finish",
    )(*[pltpu.with_memory_space_constraint(result, VMEM) for result in results])


def solution(mesh):
    in_specs = (
        P(None, "gx", "gy", None, None),
        P(None, "gx", "gy", None, None),
        P("gx", "gy", None, None),
        P("gx", "gy", None, None),
        P("gx", "gy", None),
    )
    out_specs = (
        P("gx", "gy", None, None),
        P(None, "gx", "gy", None, None),
        P("gx", "gy", None, None),
    )
    return jax.shard_map(shards, mesh=mesh, in_specs=in_specs, out_specs=out_specs, check_vma=False)
```

```python
import functools
import math

import jax
import jax.numpy as jnp
from jax import lax
from jax.experimental import pallas as pl
from jax.experimental.pallas import tpu as pltpu
from jax.sharding import PartitionSpec as P

SMOOTHING = 0.5
NORMALISE = 1.0 / (math.pi * 0.125)
ADIABATIC = 5.0 / 3.0
VISC_ALPHA = 1.0
VISC_BETA = 2.0
SOFTENING = 0.01
TINY = 1e-30
VMEM = pltpu.VMEM
MESH = pl.DeviceIdType.MESH
DIRECTIONS = [(dx, dy) for dx in (-1, 0, 1) for dy in (-1, 0, 1) if (dx, dy) != (0, 0)]
DEPTH = 64
SUMS = 5
VMEM_GRANT = 16 * 2**20
CHUNK = 64
UNITS = 2


def edge(step, count):
    if step == 0:
        return (0, 1, count)
    if step == 1:
        return (count - 1, 0, 1)
    return (0, count + 1, 1)


def start_copies(peers, own_ref, out_ref, count_x, count_y, send_sem, recv_sem):
    copies = []
    for k, (dx, dy) in enumerate(DIRECTIONS):
        from_x, to_x, width_x = edge(dx, count_x)
        from_y, to_y, width_y = edge(dy, count_y)
        copy = pltpu.make_async_remote_copy(
            src_ref=own_ref.at[pl.ds(from_x, width_x), pl.ds(from_y, width_y)],
            dst_ref=out_ref.at[pl.ds(to_x, width_x), pl.ds(to_y, width_y)],
            send_sem=send_sem.at[k],
            recv_sem=recv_sem.at[k],
            device_id=peers[k],
            device_id_type=MESH,
        )
        copy.start()
        copies.append(copy)
    return copies


def split(values):
    high = values.astype(jnp.bfloat16).astype(jnp.float32)
    rest = values - high
    middle = rest.astype(jnp.bfloat16).astype(jnp.float32)
    return high, middle, rest - middle


def look_up(step, values):
    result = step + values[0]
    for k in range(1, len(values)):
        jump = values[k] - values[k - 1] - 1
        if jump:
            result = result + jnp.where(step >= k, jump, 0)
    return result


def fold(values, slots):
    total = values[:, 0:slots]
    for k in range(slots, values.shape[1], slots):
        total = total + values[:, k : k + slots]
    return total


def thermal_rows(energy, rho):
    pressure = (ADIABATIC - 1.0) * energy / rho
    sound = jnp.sqrt(ADIABATIC * (ADIABATIC - 1.0) * energy) * (0.5 * VISC_ALPHA / VISC_BETA)
    dense = rho * (0.5 / VISC_BETA)
    rows = lax.broadcasted_iota(jnp.int32, (8, energy.shape[1]), 0)
    return jnp.where(rows == 0, pressure, jnp.where(rows == 1, sound, jnp.where(rows == 2, dense, 0.0)))


def pairs_between(own, columns, size_y):
    result = []
    for near_x, near_y in columns:
        for column, (x, y) in enumerate(own):
            if abs(near_x - x) <= 1 and abs(near_y - y) <= 1:
                result.append((column, near_x * size_y + near_y))
    return sorted(result)


def split_own(own, size_y):
    pairs = pairs_between(own, own, size_y)
    return pairs[::2], pairs[1::2]


def wide(ref, units, row):
    return jnp.concatenate([ref[unit, row : row + 1, :] for unit in units], axis=1)


def multiply(left, right_ref, units):
    right = jnp.concatenate([right_ref[unit] for unit in units], axis=1)
    return jnp.dot(left, right, preferred_element_type=jnp.float32)


def add_forces(column, units, count, span, near_row_ref, warm_row_ref, mine_ref, pair_ref, sums_ref):
    slots = near_row_ref.shape[2]
    mass = wide(near_row_ref, units, 6)
    spots = [wide(near_row_ref, units, f) for f in range(3)]
    near_pressure, near_sound, near_dense = (wide(warm_row_ref, units, k) for k in range(3))
    for first in range(0, count, CHUNK):
        at = slice(first, first + CHUNK)
        dist, approach = pair_ref[at, :], pair_ref[span + first : span + first + CHUNK, :]
        pressure, sound, dense = (
            jnp.concatenate([mine_ref[column, k, at, :]] * len(units), axis=1) for k in range(3)
        )
        safe = jnp.minimum(jnp.maximum(dist, TINY), 1.0)
        inverse = lax.rsqrt(safe)
        half = safe * inverse
        slope = jnp.minimum(inverse, 2.0) + jnp.maximum(half - 2.0, -3.0 * half)
        mu = jnp.minimum(approach, 0.0) / (dist + 0.25 * SOFTENING)
        own_push = mu * (mu - (sound + near_sound)) / (dense + near_dense) + pressure
        weight = mass * slope
        push = weight * (own_push + near_pressure)
        heat = weight * (own_push + pressure) * approach
        terms = [push] + [push * spot for spot in spots] + [heat]
        for k, term in enumerate(terms):
            sums_ref[column, k, at, :] = sums_ref[column, k, at, :] + fold(term, slots)


def sph_kernel(
    size_gx, size_gy, offsets_hbm, velocity_hbm, mass_hbm, energy_hbm, counts_hbm,
    left_ref, right_ref, near_row_ref, warm_row_ref, mine_ref, sums_ref, safe_ref,
    offsets_ref, velocity_ref, mass_ref, energy_ref, counts_ref, own_ref, ext_ref, near_ref, total_ref, dist_ref, pair_ref,
    send_sem, recv_sem, rho_send, rho_recv, in_sem,
):
    count_x, count_y, layers, _, slots = own_ref.shape
    size_y = count_y + 2
    span = layers * slots
    own = [(x, y) for x in range(1, count_x + 1) for y in range(1, count_y + 1)]
    my_x, my_y = lax.axis_index("gx"), lax.axis_index("gy")
    barrier = pltpu.get_barrier_semaphore()
    peers = []
    for dx, dy in DIRECTIONS:
        peers.append(
            (lax.rem(my_x + dx + size_gx, size_gx), lax.rem(my_y + dy + size_gy, size_gy))
        )
    for peer in peers:
        pl.semaphore_signal(barrier, inc=1, device_id=peer, device_id_type=MESH)
    sources = (offsets_hbm, velocity_hbm, mass_hbm, energy_hbm, counts_hbm)
    targets = (offsets_ref, velocity_ref, mass_ref, energy_ref, counts_ref)
    loads = [pltpu.make_async_copy(a, b, in_sem.at[k]) for k, (a, b) in enumerate(zip(sources, targets))]
    for load in loads:
        load.start()
    for load in loads:
        load.wait()
    lane = lax.broadcasted_iota(jnp.int32, (1, slots), 1)
    lanes8 = lax.broadcasted_iota(jnp.int32, (8, slots), 1)
    rows8 = lax.broadcasted_iota(jnp.int32, (8, slots), 0)
    for x in range(count_x):
        for y in range(count_y):
            for z in range(layers):
                at = slice(z, z + 1)
                for f in range(3):
                    height = float(z) if f == 2 else 0.0
                    own_ref[x, y, z, f : f + 1, :] = offsets_ref[f, x, y, at, :] + height
                    own_ref[x, y, z, 3 + f : 4 + f, :] = velocity_ref[f, x, y, at, :]
                own_ref[x, y, z, 6:7, :] = jnp.where(
                    lane < counts_ref[x, y, z], mass_ref[x, y, at, :], 0.0
                )
                own_ref[x, y, z, 7:8, :] = energy_ref[x, y, at, :]
            below = counts_ref[x, y, 0]
            moved = own_ref[x, y, 1]
            step = 1
            while step < slots:
                moved = jnp.where(jnp.bitwise_and(below, step) > 0, pltpu.roll(moved, step, 1), moved)
                step *= 2
            under = lanes8 < below
            own_ref[x, y, 0] = jnp.where(under, own_ref[x, y, 0], moved)
            own_ref[x, y, 1] = jnp.where(jnp.logical_or(under, rows8 != 6), moved, 0.0)

    rows = lax.broadcasted_iota(jnp.int32, (8, slots), 0)
    none = jnp.zeros((8, slots), jnp.float32)
    inner_x, inner_y = range(1, count_x + 1), range(1, count_y + 1)
    low_first = my_y > 0
    side = jnp.where(low_first, 0, count_y + 1)
    other_side = jnp.where(low_first, count_y + 1, 0)

    def place(cell, x, y):
        middle_y = jnp.asarray(y, jnp.float32) - (1.0 + 0.5 * count_y)
        shift = jnp.where(
            rows == 0, float(x - 1) - 0.5 * count_x, jnp.where(rows == 1, middle_y, -0.5 * layers)
        )
        placed = jnp.where(rows < 3, (cell + shift) * (1.0 / SMOOTHING), cell)
        other = pltpu.roll(placed, 5, 0)
        length = jnp.sum(jnp.where(rows < 3, placed * placed, 0.0), axis=0, keepdims=True)
        moving = jnp.sum(jnp.where(rows < 3, placed * other, 0.0), axis=0, keepdims=True)
        return placed, other, length, moving

    def enter(placed, length, moving, x, y, z):
        unit = (x * size_y + y) * layers + z
        features = jnp.where(rows < 6, placed, jnp.where(rows == 6, length, moving))
        high, middle, low = split(features)
        ones = jnp.where(rows < 3, 1.0, 0.0)
        tile = jnp.concatenate([high, high, high, middle, middle, low, ones, none], axis=0)
        right_ref[unit] = tile.astype(jnp.bfloat16)
        near_row_ref[unit] = placed

    def enter_near(x, y, z):
        placed, _, length, moving = place(ext_ref[x, y, z], x, y)
        enter(placed, length, moving, x, y, z)

    def coefficients(terms, constant):
        high, middle, low = split(terms)
        parts = split(constant)
        last = jnp.where(
            rows == 0, parts[0], jnp.where(rows == 1, parts[1], jnp.where(rows == 2, parts[2], 0.0))
        )
        tile = jnp.concatenate([high, middle, low, high, middle, high, last, none], axis=0)
        return tile.T.astype(jnp.bfloat16)

    def units_of(block):
        return [block * layers + z for z in range(layers)]

    def products(column, block, count):
        return multiply(left_ref[column, 0:count, 0:DEPTH], right_ref, units_of(block))

    def sweep(pairs, count, held_ref, process):
        tables = pairs if isinstance(pairs, tuple) else (pairs,)
        length = len(tables[0])

        def at(step):
            found = [tuple(look_up(step, [pair[k] for pair in table]) for k in range(2)) for table in tables]
            if len(found) == 1:
                return found[0]
            return tuple(jnp.where(low_first, a, b) for a, b in zip(*found))

        def step_zero(step):
            found = [table[min(step, length - 1)] for table in tables]
            if len(found) == 1:
                return tuple(jnp.int32(value) for value in found[0])
            return tuple(jnp.where(low_first, a, b) for a, b in zip(*found))

        start = step_zero(0) + step_zero(1)
        held_ref[...] = products(start[0], start[1], count)

        def body(step, carry):
            column, block, next_column, next_block = carry
            following = products(next_column, next_block, count)
            process(column, block)
            held_ref[...] = following
            return (next_column, next_block) + at(jnp.minimum(step + 2, length - 1))

        lax.fori_loop(0, length, body, start, unroll=2)

    def density_step(column, block):
        mass = wide(near_row_ref, units_of(block), 6)
        for first in range(0, span, CHUNK):
            at = slice(first, first + CHUNK)
            dist = jnp.maximum(dist_ref[at, :], TINY)
            outer = jnp.maximum(1.0 - dist * lax.rsqrt(dist), 0.0)
            kernel = jnp.where(dist < 0.25, 0.5 - 3.0 * (dist * outer), outer * outer * outer)
            total_ref[column, at, :] = total_ref[column, at, :] + fold(kernel * mass, slots)

    def force_step(column, block):
        add_forces(
            column, units_of(block), span, span, near_row_ref, warm_row_ref, mine_ref, pair_ref, sums_ref
        )

    across = [(x, y) for x in (0, count_x + 1) for y in inner_y]
    low_side = [(x, 0) for x in range(count_x + 2)]
    high_side = [(x, count_y + 1) for x in range(count_x + 2)]

    def wait_side(which, copies):
        for copy, (_, dy) in zip(copies, DIRECTIONS):
            if dy == which:
                copy.wait_recv()

    def block_of(x, y):
        return x * size_y + y

    def pairs_with(columns):
        return pairs_between(own, columns, size_y)

    def start_own():
        for column, (x, y) in enumerate(own):
            for z in range(layers):
                placed, other, length, moving = place(own_ref[x - 1, y - 1, z], x, y)
                enter(placed, length, moving, x, y, z)
                gap = jnp.where(rows < 3, -0.5 * placed, jnp.where(rows == 6, 0.25, 0.0))
                left_ref[column, pl.ds(z * slots, slots), 0:DEPTH] = coefficients(gap, 0.25 * length)
                swapped = jnp.where(rows < 3, other, pltpu.roll(placed, 3, 0))
                rate = jnp.where(rows < 6, -0.25 * swapped, jnp.where(rows == 7, 0.25, 0.0))
                left_ref[column, pl.ds(span + z * slots, slots), 0:DEPTH] = coefficients(rate, 0.25 * moving)
        total_ref[...] = jnp.zeros_like(total_ref)
        spare = right_ref.shape[0] - 1
        right_ref[spare] = jnp.zeros(right_ref.shape[1:], jnp.bfloat16)
        near_row_ref[spare] = none
        warm_row_ref[spare] = none + 1.0
        sums_ref[...] = jnp.zeros_like(sums_ref)
        sweep(pairs_with(own), span, dist_ref, density_step)

    first_rows = my_y < 2
    pl.when(first_rows)(start_own)
    pl.semaphore_wait(barrier, len(peers))
    copies = start_copies(peers, own_ref, ext_ref, count_x, count_y, send_sem, recv_sem)
    pl.when(jnp.logical_not(first_rows))(start_own)

    wait_side(0, copies)
    pl.when(low_first)(lambda: wait_side(1, copies))
    pl.when(jnp.logical_not(low_first))(lambda: wait_side(-1, copies))
    for x, y in across:
        for z in range(layers):
            enter_near(x, y, z)
    for x in range(count_x + 2):
        for z in range(layers):
            enter_near(x, side, z)
    sweep(
        (pairs_with(across) + pairs_with(low_side), pairs_with(across) + pairs_with(high_side)),
        span, dist_ref, density_step,
    )
    pl.when(low_first)(lambda: wait_side(-1, copies))
    pl.when(jnp.logical_not(low_first))(lambda: wait_side(1, copies))
    for x in range(count_x + 2):
        for z in range(layers):
            enter_near(x, other_side, z)
    sweep((pairs_with(high_side), pairs_with(low_side)), span, dist_ref, density_step)
    for column, (x, y) in enumerate(own):
        for z in range(layers):
            total = total_ref[column, z * slots : (z + 1) * slots, :].T
            row = jnp.sum(total, axis=0, keepdims=True) * (2.0 * NORMALISE)
            held = own_ref[x - 1, y - 1, z, 6:7, :] > 0.0
            safe_ref[x - 1, y - 1, z : z + 1, :] = jnp.where(held, row, 1.0)
    rho_copies = start_copies(peers, safe_ref, near_ref, count_x, count_y, rho_send, rho_recv)
    for copy in copies:
        copy.wait_send()
    for column, (x, y) in enumerate(own):
        for z in range(layers):
            warm = thermal_rows(own_ref[x - 1, y - 1, z, 7:8, :], safe_ref[x - 1, y - 1, z : z + 1, :])
            warm_row_ref[block_of(x, y) * layers + z] = warm
            turned = jnp.concatenate([warm] + [none] * 7, axis=0).T
            for k in range(3):
                mine_ref[column, k, pl.ds(z * slots, slots), :] = jnp.broadcast_to(
                    turned[:, k : k + 1], (slots, slots)
                )
    sweep(split_own(own, size_y)[0], 2 * span, pair_ref, force_step)
    for copy in rho_copies:
        copy.wait()
    halo = across + low_side + high_side
    for x, y in halo:
        for z in range(layers):
            warm = thermal_rows(ext_ref[x, y, z, 7:8, :], near_ref[x, y, z : z + 1, :])
            warm_row_ref[block_of(x, y) * layers + z] = warm


def force_kernel(
    shape, counts_hbm, left_ref, right_ref, near_row_ref, warm_row_ref, mine_ref, start_ref, safe_ref,
    density_out, accel_out, heat_out, counts_ref, sums_ref, pair_ref, table_ref, length_ref, in_sem,
):
    count_x, count_y, layers, slots = shape
    size_y = count_y + 2
    span = layers * slots
    own = [(x, y) for x in range(1, count_x + 1) for y in range(1, count_y + 1)]
    columns = [(x, y) for x in range(count_x + 2) for y in range(size_y)]
    spare = len(columns) * layers
    done = split_own(own, size_y)[0]
    load = pltpu.make_async_copy(counts_hbm, counts_ref, in_sem)
    load.start()
    sums_ref[...] = start_ref[...]
    second = []
    for block in range(len(columns)):
        held = jnp.sum(near_row_ref[block * layers + 1, 6:7, :])
        second.append(jnp.where(held > 0.0, 1, 0))
    for column, (x, y) in enumerate(own):
        length = jnp.int32(0)
        for pair in pairs_between([(x, y)], columns, size_y):
            if (column, pair[1]) not in done:
                table_ref[column, length] = pair[1] * layers
                table_ref[column, length + 1] = pair[1] * layers + 1
                length = length + 1 + second[pair[1]]
        for k in range(2 * UNITS):
            table_ref[column, length + k] = spare
        length_ref[column] = length

    load.wait()

    def run(column, count):
        def keep(units):
            pair_ref[0:count, :] = multiply(left_ref[column, 0:count, 0:DEPTH], right_ref, units)
            pair_ref[span : span + count, :] = multiply(
                left_ref[column, span : span + count, 0:DEPTH], right_ref, units
            )

        def units_at(step):
            return tuple(table_ref[column, step * UNITS + k] for k in range(UNITS))

        keep(units_at(0))

        def body(step, carry):
            units, following = carry
            near = multiply(left_ref[column, 0:count, 0:DEPTH], right_ref, following)
            fast = multiply(left_ref[column, span : span + count, 0:DEPTH], right_ref, following)
            add_forces(
                column, units, count, span, near_row_ref, warm_row_ref, mine_ref, pair_ref, sums_ref
            )
            pair_ref[0:count, :] = near
            pair_ref[span : span + count, :] = fast
            return following, units_at(jnp.minimum(step + 2, steps))

        steps = (length_ref[column] + (UNITS - 1)) // UNITS
        lax.fori_loop(0, steps, body, (units_at(0), units_at(1)))

    def each(column, carry):
        x, y = column // count_y, lax.rem(column, count_y)
        held = counts_ref[x, y, 0] + counts_ref[x, y, 1]
        for count in range(CHUNK, span + 1, CHUNK):
            pl.when(jnp.logical_and(held > count - CHUNK, held <= count))(functools.partial(run, column, count))
        return carry

    lax.fori_loop(0, len(own), each, 0)
    factor = 1.5 * NORMALISE / SMOOTHING
    rows = lax.broadcasted_iota(jnp.int32, (8, slots), 0)
    lane = lax.broadcasted_iota(jnp.int32, (8, slots), 1)
    for column, (x, y) in enumerate(own):
        packed = []
        for z in range(layers):
            at = slice(z * slots, (z + 1) * slots)
            sums = [jnp.sum(sums_ref[column, k, at, :].T, axis=0, keepdims=True) for k in range(SUMS)]
            unit = (x * size_y + y) * layers + z
            result = jnp.broadcast_to(safe_ref[x - 1, y - 1, z : z + 1, :], (8, slots))
            for f in range(3):
                value = (near_row_ref[unit, f : f + 1, :] * sums[0] - sums[1 + f]) * factor
                result = jnp.where(rows == f, value, result)
            packed.append(jnp.where(rows == 3, sums[4] * (-2.0 * factor), result))
        below = counts_ref[x - 1, y - 1, 0]
        back = jnp.where(below == slots, 0, slots - below)
        lower, upper = pltpu.roll(packed[0], back, 1), pltpu.roll(packed[1], back, 1)
        cells = [packed[0], jnp.where(lane < slots - below, lower, upper)]
        for z in range(layers):
            cell = jnp.where(lane < counts_ref[x - 1, y - 1, z], cells[z], 0.0)
            for f in range(3):
                accel_out[f, x - 1, y - 1, z : z + 1, :] = cell[f : f + 1]
            heat_out[x - 1, y - 1, z : z + 1, :] = cell[3:4]
            density_out[x - 1, y - 1, z : z + 1, :] = cell[4:5]


def shards(offsets, velocity, mass, energy, counts):
    slots = mass.shape[-1]
    count_x, count_y, layers = mass.shape[:3]
    wide_x, wide_y = count_x + 2, count_y + 2
    own = count_x * count_y
    span = layers * slots
    vmem = pl.BlockSpec(memory_space=VMEM)
    units = wide_x * wide_y * layers + 1
    shapes = (mass.shape, (3,) + mass.shape, mass.shape)
    between = [
        VMEM((own, 2 * span, 128), jnp.bfloat16),
        VMEM((units, DEPTH, slots), jnp.bfloat16),
        VMEM((units, 8, slots), jnp.float32),
        VMEM((units, 8, slots), jnp.float32),
        VMEM((own, 3, span, slots), jnp.float32),
        VMEM((own, SUMS, span, slots), jnp.float32),
        VMEM((count_x, count_y, layers, slots), jnp.float32),
    ]
    hbm = pl.BlockSpec(memory_space=pltpu.HBM)
    inputs = [
        pltpu.with_memory_space_constraint(x, pltpu.HBM)
        for x in (offsets, velocity, mass, energy, counts)
    ]
    sems = pltpu.SemaphoreType.DMA((len(DIRECTIONS),))
    cell_shape = (layers, 8, slots)
    results = pl.pallas_call(
        functools.partial(sph_kernel, lax.axis_size("gx"), lax.axis_size("gy")),
        out_shape=between,
        in_specs=[hbm] * 5,
        out_specs=[vmem] * len(between),
        scratch_shapes=[
            VMEM(offsets.shape, jnp.float32),
            VMEM(velocity.shape, jnp.float32),
            VMEM(mass.shape, jnp.float32),
            VMEM(energy.shape, jnp.float32),
            pltpu.SMEM(counts.shape, jnp.int32),
            VMEM((count_x, count_y) + cell_shape, jnp.float32),
            VMEM((wide_x, wide_y) + cell_shape, jnp.float32),
            VMEM((wide_x, wide_y, layers, slots), jnp.float32),
            VMEM((own, span, slots), jnp.float32),
            VMEM((span, span), jnp.float32),
            VMEM((2 * span, span), jnp.float32),
            sems,
            sems,
            sems,
            sems,
            pltpu.SemaphoreType.DMA((5,)),
        ],
        compiler_params=pltpu.CompilerParams(
            collective_id=0, has_side_effects=True, vmem_limit_bytes=VMEM_GRANT
        ),
        name="sph",
    )(*inputs)
    return pl.pallas_call(
        functools.partial(force_kernel, mass.shape),
        out_shape=[jax.ShapeDtypeStruct(shape, jnp.float32) for shape in shapes],
        in_specs=[hbm] + [vmem] * len(between),
        out_specs=[vmem] * 3,
        scratch_shapes=[
            pltpu.SMEM(counts.shape, jnp.int32),
            VMEM((own, SUMS, span, slots), jnp.float32),
            VMEM((2 * span, UNITS * slots), jnp.float32),
            pltpu.SMEM((own, 9 * layers + 2 * UNITS), jnp.int32),
            pltpu.SMEM((own,), jnp.int32),
            pltpu.SemaphoreType.DMA,
        ],
        compiler_params=pltpu.CompilerParams(vmem_limit_bytes=VMEM_GRANT),
        name="force",
    )(inputs[4], *[pltpu.with_memory_space_constraint(result, VMEM) for result in results])


def solution(mesh):
    in_specs = (
        P(None, "gx", "gy", None, None),
        P(None, "gx", "gy", None, None),
        P("gx", "gy", None, None),
        P("gx", "gy", None, None),
        P("gx", "gy", None),
    )
    out_specs = (
        P("gx", "gy", None, None),
        P(None, "gx", "gy", None, None),
        P("gx", "gy", None, None),
    )
    return jax.shard_map(shards, mesh=mesh, in_specs=in_specs, out_specs=out_specs, check_vma=False)
```

```python
import functools
import math

import jax
import jax.numpy as jnp
from jax import lax
from jax.experimental import pallas as pl
from jax.experimental.pallas import tpu as pltpu
from jax.sharding import PartitionSpec as P

SMOOTHING = 0.5
NORMALISE = 1.0 / (math.pi * 0.125)
ADIABATIC = 5.0 / 3.0
VISC_ALPHA = 1.0
VISC_BETA = 2.0
SOFTENING = 0.01
TINY = 1e-30
VMEM = pltpu.VMEM
MESH = pl.DeviceIdType.MESH
DIRECTIONS = [(dx, dy) for dx in (-1, 0, 1) for dy in (-1, 0, 1) if (dx, dy) != (0, 0)]
DEPTH = 64
SUMS = 5
VMEM_GRANT = 16 * 2**20
CHUNK = 32
UNITS = 2


def edge(step, count):
    if step == 0:
        return (0, 1, count)
    if step == 1:
        return (count - 1, 0, 1)
    return (0, count + 1, 1)


def start_copies(peers, own_ref, out_ref, count_x, count_y, send_sem, recv_sem):
    copies = []
    for k, (dx, dy) in enumerate(DIRECTIONS):
        from_x, to_x, width_x = edge(dx, count_x)
        from_y, to_y, width_y = edge(dy, count_y)
        copy = pltpu.make_async_remote_copy(
            src_ref=own_ref.at[pl.ds(from_x, width_x), pl.ds(from_y, width_y)],
            dst_ref=out_ref.at[pl.ds(to_x, width_x), pl.ds(to_y, width_y)],
            send_sem=send_sem.at[k],
            recv_sem=recv_sem.at[k],
            device_id=peers[k],
            device_id_type=MESH,
        )
        copy.start()
        copies.append(copy)
    return copies


def split(values):
    high = values.astype(jnp.bfloat16).astype(jnp.float32)
    rest = values - high
    middle = rest.astype(jnp.bfloat16).astype(jnp.float32)
    return high, middle, rest - middle


def look_up(step, values):
    result = step + values[0]
    for k in range(1, len(values)):
        jump = values[k] - values[k - 1] - 1
        if jump:
            result = result + jnp.where(step >= k, jump, 0)
    return result


def fold(values, slots):
    total = values[:, 0:slots]
    for k in range(slots, values.shape[1], slots):
        total = total + values[:, k : k + slots]
    return total


def thermal_rows(energy, rho):
    pressure = (ADIABATIC - 1.0) * energy / rho
    sound = jnp.sqrt(ADIABATIC * (ADIABATIC - 1.0) * energy) * (0.5 * VISC_ALPHA / VISC_BETA)
    dense = rho * (0.5 / VISC_BETA)
    rows = lax.broadcasted_iota(jnp.int32, (8, energy.shape[1]), 0)
    return jnp.where(rows == 0, pressure, jnp.where(rows == 1, sound, jnp.where(rows == 2, dense, 0.0)))


def pairs_between(own, columns, size_y):
    result = []
    for near_x, near_y in columns:
        for column, (x, y) in enumerate(own):
            if abs(near_x - x) <= 1 and abs(near_y - y) <= 1:
                result.append((column, near_x * size_y + near_y))
    return sorted(result)


def split_own(own, size_y):
    pairs = pairs_between(own, own, size_y)
    return pairs[::2], pairs[1::2]


def wide(ref, units, row):
    return jnp.concatenate([ref[unit, row : row + 1, :] for unit in units], axis=1)


def multiply(left, right_ref, units):
    right = jnp.concatenate([right_ref[unit] for unit in units], axis=1)
    return jnp.dot(left, right, preferred_element_type=jnp.float32)


def add_forces(column, units, count, span, near_row_ref, warm_row_ref, mine_ref, pair_ref, sums_ref):
    slots = near_row_ref.shape[2]
    mass = wide(near_row_ref, units, 6)
    spots = [wide(near_row_ref, units, f) for f in range(3)]
    near_pressure, near_sound, near_dense = (wide(warm_row_ref, units, k) for k in range(3))
    for first in range(0, count, CHUNK):
        at = slice(first, first + CHUNK)
        dist, approach = pair_ref[at, :], pair_ref[span + first : span + first + CHUNK, :]
        pressure, sound, dense = (
            jnp.concatenate([mine_ref[column, k, at, :]] * len(units), axis=1) for k in range(3)
        )
        safe = jnp.minimum(jnp.maximum(dist, TINY), 1.0)
        inverse = lax.rsqrt(safe)
        half = safe * inverse
        slope = jnp.minimum(inverse, 2.0) + jnp.maximum(half - 2.0, -3.0 * half)
        mu = jnp.minimum(approach, 0.0) / (dist + 0.25 * SOFTENING)
        own_push = mu * (mu - (sound + near_sound)) / (dense + near_dense) + pressure
        weight = mass * slope
        push = weight * (own_push + near_pressure)
        heat = weight * (own_push + pressure) * approach
        terms = [push] + [push * spot for spot in spots] + [heat]
        for k, term in enumerate(terms):
            sums_ref[column, k, at, :] = sums_ref[column, k, at, :] + fold(term, slots)


def sph_kernel(
    size_gx, size_gy, offsets_hbm, velocity_hbm, mass_hbm, energy_hbm, counts_hbm,
    left_ref, right_ref, near_row_ref, warm_row_ref, mine_ref, sums_ref, safe_ref,
    offsets_ref, velocity_ref, mass_ref, energy_ref, counts_ref, own_ref, ext_ref, near_ref, total_ref, dist_ref, pair_ref,
    send_sem, recv_sem, rho_send, rho_recv, in_sem,
):
    count_x, count_y, layers, _, slots = own_ref.shape
    size_y = count_y + 2
    span = layers * slots
    own = [(x, y) for x in range(1, count_x + 1) for y in range(1, count_y + 1)]
    my_x, my_y = lax.axis_index("gx"), lax.axis_index("gy")
    barrier = pltpu.get_barrier_semaphore()
    peers = []
    for dx, dy in DIRECTIONS:
        peers.append(
            (lax.rem(my_x + dx + size_gx, size_gx), lax.rem(my_y + dy + size_gy, size_gy))
        )
    for peer in peers:
        pl.semaphore_signal(barrier, inc=1, device_id=peer, device_id_type=MESH)
    sources = (offsets_hbm, velocity_hbm, mass_hbm, energy_hbm, counts_hbm)
    targets = (offsets_ref, velocity_ref, mass_ref, energy_ref, counts_ref)
    loads = [pltpu.make_async_copy(a, b, in_sem.at[k]) for k, (a, b) in enumerate(zip(sources, targets))]
    for load in loads:
        load.start()
    for load in loads:
        load.wait()
    lane = lax.broadcasted_iota(jnp.int32, (1, slots), 1)
    lanes8 = lax.broadcasted_iota(jnp.int32, (8, slots), 1)
    rows8 = lax.broadcasted_iota(jnp.int32, (8, slots), 0)
    for x in range(count_x):
        for y in range(count_y):
            for z in range(layers):
                at = slice(z, z + 1)
                for f in range(3):
                    height = float(z) if f == 2 else 0.0
                    own_ref[x, y, z, f : f + 1, :] = offsets_ref[f, x, y, at, :] + height
                    own_ref[x, y, z, 3 + f : 4 + f, :] = velocity_ref[f, x, y, at, :]
                own_ref[x, y, z, 6:7, :] = jnp.where(
                    lane < counts_ref[x, y, z], mass_ref[x, y, at, :], 0.0
                )
                own_ref[x, y, z, 7:8, :] = energy_ref[x, y, at, :]
            below = counts_ref[x, y, 0]
            moved = own_ref[x, y, 1]
            step = 1
            while step < slots:
                moved = jnp.where(jnp.bitwise_and(below, step) > 0, pltpu.roll(moved, step, 1), moved)
                step *= 2
            under = lanes8 < below
            own_ref[x, y, 0] = jnp.where(under, own_ref[x, y, 0], moved)
            own_ref[x, y, 1] = jnp.where(jnp.logical_or(under, rows8 != 6), moved, 0.0)

    rows = lax.broadcasted_iota(jnp.int32, (8, slots), 0)
    none = jnp.zeros((8, slots), jnp.float32)
    inner_x, inner_y = range(1, count_x + 1), range(1, count_y + 1)
    low_first = my_y > 1
    side = jnp.where(low_first, 0, count_y + 1)
    other_side = jnp.where(low_first, count_y + 1, 0)

    def place(cell, x, y):
        middle_y = jnp.asarray(y, jnp.float32) - (1.0 + 0.5 * count_y)
        shift = jnp.where(
            rows == 0, float(x - 1) - 0.5 * count_x, jnp.where(rows == 1, middle_y, -0.5 * layers)
        )
        placed = jnp.where(rows < 3, (cell + shift) * (1.0 / SMOOTHING), cell)
        other = pltpu.roll(placed, 5, 0)
        length = jnp.sum(jnp.where(rows < 3, placed * placed, 0.0), axis=0, keepdims=True)
        moving = jnp.sum(jnp.where(rows < 3, placed * other, 0.0), axis=0, keepdims=True)
        return placed, other, length, moving

    def enter(placed, length, moving, x, y, z):
        unit = (x * size_y + y) * layers + z
        features = jnp.where(rows < 6, placed, jnp.where(rows == 6, length, moving))
        high, middle, low = split(features)
        ones = jnp.where(rows < 3, 1.0, 0.0)
        tile = jnp.concatenate([high, high, high, middle, middle, low, ones, none], axis=0)
        right_ref[unit] = tile.astype(jnp.bfloat16)
        near_row_ref[unit] = placed

    def enter_near(x, y, z):
        placed, _, length, moving = place(ext_ref[x, y, z], x, y)
        enter(placed, length, moving, x, y, z)

    def coefficients(terms, constant):
        high, middle, low = split(terms)
        parts = split(constant)
        last = jnp.where(
            rows == 0, parts[0], jnp.where(rows == 1, parts[1], jnp.where(rows == 2, parts[2], 0.0))
        )
        tile = jnp.concatenate([high, middle, low, high, middle, high, last, none], axis=0)
        return tile.T.astype(jnp.bfloat16)

    def units_of(block):
        return [block * layers + z for z in range(layers)]

    def products(column, block, count):
        return multiply(left_ref[column, 0:count, 0:DEPTH], right_ref, units_of(block))

    def sweep(pairs, count, held_ref, process):
        tables = pairs if isinstance(pairs, tuple) else (pairs,)
        length = len(tables[0])

        def at(step):
            found = [tuple(look_up(step, [pair[k] for pair in table]) for k in range(2)) for table in tables]
            if len(found) == 1:
                return found[0]
            return tuple(jnp.where(low_first, a, b) for a, b in zip(*found))

        def step_zero(step):
            found = [table[min(step, length - 1)] for table in tables]
            if len(found) == 1:
                return tuple(jnp.int32(value) for value in found[0])
            return tuple(jnp.where(low_first, a, b) for a, b in zip(*found))

        start = step_zero(0) + step_zero(1)
        held_ref[...] = products(start[0], start[1], count)

        def body(step, carry):
            column, block, next_column, next_block = carry
            following = products(next_column, next_block, count)
            process(column, block)
            held_ref[...] = following
            return (next_column, next_block) + at(jnp.minimum(step + 2, length - 1))

        lax.fori_loop(0, length, body, start, unroll=2)

    def density_step(column, block):
        mass = wide(near_row_ref, units_of(block), 6)
        for first in range(0, span, CHUNK):
            at = slice(first, first + CHUNK)
            dist = jnp.maximum(dist_ref[at, :], TINY)
            outer = jnp.maximum(1.0 - dist * lax.rsqrt(dist), 0.0)
            kernel = jnp.where(dist < 0.25, 0.5 - 3.0 * (dist * outer), outer * outer * outer)
            total_ref[column, at, :] = total_ref[column, at, :] + fold(kernel * mass, slots)

    def force_step(column, block):
        add_forces(
            column, units_of(block), span, span, near_row_ref, warm_row_ref, mine_ref, pair_ref, sums_ref
        )

    across = [(x, y) for x in (0, count_x + 1) for y in inner_y]
    low_side = [(x, 0) for x in range(count_x + 2)]
    high_side = [(x, count_y + 1) for x in range(count_x + 2)]

    def wait_side(which, copies):
        for copy, (_, dy) in zip(copies, DIRECTIONS):
            if dy == which:
                copy.wait_recv()

    def block_of(x, y):
        return x * size_y + y

    def pairs_with(columns):
        return pairs_between(own, columns, size_y)

    def start_own():
        for column, (x, y) in enumerate(own):
            for z in range(layers):
                placed, other, length, moving = place(own_ref[x - 1, y - 1, z], x, y)
                enter(placed, length, moving, x, y, z)
                gap = jnp.where(rows < 3, -0.5 * placed, jnp.where(rows == 6, 0.25, 0.0))
                left_ref[column, pl.ds(z * slots, slots), 0:DEPTH] = coefficients(gap, 0.25 * length)
                swapped = jnp.where(rows < 3, other, pltpu.roll(placed, 3, 0))
                rate = jnp.where(rows < 6, -0.25 * swapped, jnp.where(rows == 7, 0.25, 0.0))
                left_ref[column, pl.ds(span + z * slots, slots), 0:DEPTH] = coefficients(rate, 0.25 * moving)
        total_ref[...] = jnp.zeros_like(total_ref)
        spare = right_ref.shape[0] - 1
        right_ref[spare] = jnp.zeros(right_ref.shape[1:], jnp.bfloat16)
        near_row_ref[spare] = none
        warm_row_ref[spare] = none + 1.0
        sums_ref[...] = jnp.zeros_like(sums_ref)
        sweep(pairs_with(own), span, dist_ref, density_step)

    first_rows = my_y < 2
    pl.when(first_rows)(start_own)
    pl.semaphore_wait(barrier, len(peers))
    copies = start_copies(peers, own_ref, ext_ref, count_x, count_y, send_sem, recv_sem)
    pl.when(jnp.logical_not(first_rows))(start_own)

    pl.when(low_first)(lambda: wait_side(1, copies))
    pl.when(jnp.logical_not(low_first))(lambda: wait_side(-1, copies))
    for x in range(count_x + 2):
        for z in range(layers):
            enter_near(x, side, z)
    sweep((pairs_with(low_side), pairs_with(high_side)), span, dist_ref, density_step)
    wait_side(0, copies)
    for x, y in across:
        for z in range(layers):
            enter_near(x, y, z)
    sweep(pairs_with(across), span, dist_ref, density_step)
    pl.when(low_first)(lambda: wait_side(-1, copies))
    pl.when(jnp.logical_not(low_first))(lambda: wait_side(1, copies))
    for x in range(count_x + 2):
        for z in range(layers):
            enter_near(x, other_side, z)
    sweep((pairs_with(high_side), pairs_with(low_side)), span, dist_ref, density_step)
    for column, (x, y) in enumerate(own):
        for z in range(layers):
            total = total_ref[column, z * slots : (z + 1) * slots, :].T
            row = jnp.sum(total, axis=0, keepdims=True) * (2.0 * NORMALISE)
            held = own_ref[x - 1, y - 1, z, 6:7, :] > 0.0
            safe_ref[x - 1, y - 1, z : z + 1, :] = jnp.where(held, row, 1.0)
    rho_copies = start_copies(peers, safe_ref, near_ref, count_x, count_y, rho_send, rho_recv)
    for copy in copies:
        copy.wait_send()
    for column, (x, y) in enumerate(own):
        for z in range(layers):
            warm = thermal_rows(own_ref[x - 1, y - 1, z, 7:8, :], safe_ref[x - 1, y - 1, z : z + 1, :])
            warm_row_ref[block_of(x, y) * layers + z] = warm
            turned = jnp.concatenate([warm] + [none] * 7, axis=0).T
            for k in range(3):
                mine_ref[column, k, pl.ds(z * slots, slots), :] = jnp.broadcast_to(
                    turned[:, k : k + 1], (slots, slots)
                )
    sweep(split_own(own, size_y)[0], 2 * span, pair_ref, force_step)
    for copy in rho_copies:
        copy.wait()
    halo = across + low_side + high_side
    for x, y in halo:
        for z in range(layers):
            warm = thermal_rows(ext_ref[x, y, z, 7:8, :], near_ref[x, y, z : z + 1, :])
            warm_row_ref[block_of(x, y) * layers + z] = warm


def force_kernel(
    shape, counts_hbm, left_ref, right_ref, near_row_ref, warm_row_ref, mine_ref, start_ref, safe_ref,
    density_out, accel_out, heat_out, counts_ref, sums_ref, pair_ref, table_ref, length_ref, in_sem,
):
    count_x, count_y, layers, slots = shape
    size_y = count_y + 2
    span = layers * slots
    own = [(x, y) for x in range(1, count_x + 1) for y in range(1, count_y + 1)]
    columns = [(x, y) for x in range(count_x + 2) for y in range(size_y)]
    spare = len(columns) * layers
    done = split_own(own, size_y)[0]
    load = pltpu.make_async_copy(counts_hbm, counts_ref, in_sem)
    load.start()
    sums_ref[...] = start_ref[...]
    second = []
    for block in range(len(columns)):
        held = jnp.sum(near_row_ref[block * layers + 1, 6:7, :])
        second.append(jnp.where(held > 0.0, 1, 0))
    for column, (x, y) in enumerate(own):
        length = jnp.int32(0)
        for pair in pairs_between([(x, y)], columns, size_y):
            if (column, pair[1]) not in done:
                table_ref[column, length] = pair[1] * layers
                table_ref[column, length + 1] = pair[1] * layers + 1
                length = length + 1 + second[pair[1]]
        for k in range(2 * UNITS):
            table_ref[column, length + k] = spare
        length_ref[column] = length

    load.wait()

    def run(column, count):
        def products(units):
            left = [left_ref[column, first : first + count, 0:DEPTH] for first in (0, span)]
            return multiply(jnp.concatenate(left, axis=0), right_ref, units)

        def keep(found):
            pair_ref[0:count, :] = found[0:count]
            pair_ref[span : span + count, :] = found[count:]

        def units_at(step):
            return tuple(table_ref[column, step * UNITS + k] for k in range(UNITS))

        keep(products(units_at(0)))

        def body(step, carry):
            units, following = carry
            found = products(following)
            add_forces(
                column, units, count, span, near_row_ref, warm_row_ref, mine_ref, pair_ref, sums_ref
            )
            keep(found)
            return following, units_at(jnp.minimum(step + 2, steps))

        steps = (length_ref[column] + (UNITS - 1)) // UNITS
        lax.fori_loop(0, steps, body, (units_at(0), units_at(1)))

    def each(column, carry):
        x, y = column // count_y, lax.rem(column, count_y)
        held = counts_ref[x, y, 0] + counts_ref[x, y, 1]
        for count in range(CHUNK, span + 1, CHUNK):
            pl.when(jnp.logical_and(held > count - CHUNK, held <= count))(functools.partial(run, column, count))
        return carry

    lax.fori_loop(0, len(own), each, 0)
    factor = 1.5 * NORMALISE / SMOOTHING
    rows = lax.broadcasted_iota(jnp.int32, (8, slots), 0)
    lane = lax.broadcasted_iota(jnp.int32, (8, slots), 1)
    for column, (x, y) in enumerate(own):
        packed = []
        for z in range(layers):
            at = slice(z * slots, (z + 1) * slots)
            sums = [jnp.sum(sums_ref[column, k, at, :].T, axis=0, keepdims=True) for k in range(SUMS)]
            unit = (x * size_y + y) * layers + z
            result = jnp.broadcast_to(safe_ref[x - 1, y - 1, z : z + 1, :], (8, slots))
            for f in range(3):
                value = (near_row_ref[unit, f : f + 1, :] * sums[0] - sums[1 + f]) * factor
                result = jnp.where(rows == f, value, result)
            packed.append(jnp.where(rows == 3, sums[4] * (-2.0 * factor), result))
        below = counts_ref[x - 1, y - 1, 0]
        back = jnp.where(below == slots, 0, slots - below)
        lower, upper = pltpu.roll(packed[0], back, 1), pltpu.roll(packed[1], back, 1)
        cells = [packed[0], jnp.where(lane < slots - below, lower, upper)]
        for z in range(layers):
            cell = jnp.where(lane < counts_ref[x - 1, y - 1, z], cells[z], 0.0)
            for f in range(3):
                accel_out[f, x - 1, y - 1, z : z + 1, :] = cell[f : f + 1]
            heat_out[x - 1, y - 1, z : z + 1, :] = cell[3:4]
            density_out[x - 1, y - 1, z : z + 1, :] = cell[4:5]


def shards(offsets, velocity, mass, energy, counts):
    slots = mass.shape[-1]
    count_x, count_y, layers = mass.shape[:3]
    wide_x, wide_y = count_x + 2, count_y + 2
    own = count_x * count_y
    span = layers * slots
    vmem = pl.BlockSpec(memory_space=VMEM)
    units = wide_x * wide_y * layers + 1
    shapes = (mass.shape, (3,) + mass.shape, mass.shape)
    between = [
        VMEM((own, 2 * span, 128), jnp.bfloat16),
        VMEM((units, DEPTH, slots), jnp.bfloat16),
        VMEM((units, 8, slots), jnp.float32),
        VMEM((units, 8, slots), jnp.float32),
        VMEM((own, 3, span, slots), jnp.float32),
        VMEM((own, SUMS, span, slots), jnp.float32),
        VMEM((count_x, count_y, layers, slots), jnp.float32),
    ]
    hbm = pl.BlockSpec(memory_space=pltpu.HBM)
    inputs = [
        pltpu.with_memory_space_constraint(x, pltpu.HBM)
        for x in (offsets, velocity, mass, energy, counts)
    ]
    sems = pltpu.SemaphoreType.DMA((len(DIRECTIONS),))
    cell_shape = (layers, 8, slots)
    results = pl.pallas_call(
        functools.partial(sph_kernel, lax.axis_size("gx"), lax.axis_size("gy")),
        out_shape=between,
        in_specs=[hbm] * 5,
        out_specs=[vmem] * len(between),
        scratch_shapes=[
            VMEM(offsets.shape, jnp.float32),
            VMEM(velocity.shape, jnp.float32),
            VMEM(mass.shape, jnp.float32),
            VMEM(energy.shape, jnp.float32),
            pltpu.SMEM(counts.shape, jnp.int32),
            VMEM((count_x, count_y) + cell_shape, jnp.float32),
            VMEM((wide_x, wide_y) + cell_shape, jnp.float32),
            VMEM((wide_x, wide_y, layers, slots), jnp.float32),
            VMEM((own, span, slots), jnp.float32),
            VMEM((span, span), jnp.float32),
            VMEM((2 * span, span), jnp.float32),
            sems,
            sems,
            sems,
            sems,
            pltpu.SemaphoreType.DMA((5,)),
        ],
        compiler_params=pltpu.CompilerParams(
            collective_id=0, has_side_effects=True, vmem_limit_bytes=VMEM_GRANT
        ),
        name="sph",
    )(*inputs)
    return pl.pallas_call(
        functools.partial(force_kernel, mass.shape),
        out_shape=[jax.ShapeDtypeStruct(shape, jnp.float32) for shape in shapes],
        in_specs=[hbm] + [vmem] * len(between),
        out_specs=[vmem] * 3,
        scratch_shapes=[
            pltpu.SMEM(counts.shape, jnp.int32),
            VMEM((own, SUMS, span, slots), jnp.float32),
            VMEM((2 * span, UNITS * slots), jnp.float32),
            pltpu.SMEM((own, 9 * layers + 2 * UNITS), jnp.int32),
            pltpu.SMEM((own,), jnp.int32),
            pltpu.SemaphoreType.DMA,
        ],
        compiler_params=pltpu.CompilerParams(vmem_limit_bytes=VMEM_GRANT),
        name="force",
    )(inputs[4], *[pltpu.with_memory_space_constraint(result, VMEM) for result in results])


def solution(mesh):
    in_specs = (
        P(None, "gx", "gy", None, None),
        P(None, "gx", "gy", None, None),
        P("gx", "gy", None, None),
        P("gx", "gy", None, None),
        P("gx", "gy", None),
    )
    out_specs = (
        P("gx", "gy", None, None),
        P(None, "gx", "gy", None, None),
        P("gx", "gy", None, None),
    )
    return jax.shard_map(shards, mesh=mesh, in_specs=in_specs, out_specs=out_specs, check_vma=False)
```

```python
import functools
import math

import jax
import jax.numpy as jnp
from jax import lax
from jax.experimental import pallas as pl
from jax.experimental.pallas import tpu as pltpu
from jax.sharding import PartitionSpec as P

SMOOTHING = 0.5
NORMALISE = 1.0 / (math.pi * 0.125)
ADIABATIC = 5.0 / 3.0
VISC_ALPHA = 1.0
VISC_BETA = 2.0
SOFTENING = 0.01
TINY = 1e-30
VMEM = pltpu.VMEM
MESH = pl.DeviceIdType.MESH
DIRECTIONS = [(dx, dy) for dx in (-1, 0, 1) for dy in (-1, 0, 1) if (dx, dy) != (0, 0)]
DEPTH = 64
SUMS = 5
VMEM_GRANT = 16 * 2**20
CHUNK = 32
UNITS = 3


def edge(step, count):
    if step == 0:
        return (0, 1, count)
    if step == 1:
        return (count - 1, 0, 1)
    return (0, count + 1, 1)


def make_copies(peers, own_ref, out_ref, count_x, count_y, send_sem, recv_sem):
    copies = []
    for k, (dx, dy) in enumerate(DIRECTIONS):
        from_x, to_x, width_x = edge(dx, count_x)
        from_y, to_y, width_y = edge(dy, count_y)
        copy = pltpu.make_async_remote_copy(
            src_ref=own_ref.at[pl.ds(from_x, width_x), pl.ds(from_y, width_y)],
            dst_ref=out_ref.at[pl.ds(to_x, width_x), pl.ds(to_y, width_y)],
            send_sem=send_sem.at[k],
            recv_sem=recv_sem.at[k],
            device_id=peers[k],
            device_id_type=MESH,
        )
        copies.append(copy)
    return copies


def split(values):
    high = values.astype(jnp.bfloat16).astype(jnp.float32)
    rest = values - high
    middle = rest.astype(jnp.bfloat16).astype(jnp.float32)
    return high, middle, rest - middle


def look_up(step, values):
    result = step + values[0]
    for k in range(1, len(values)):
        jump = values[k] - values[k - 1] - 1
        if jump:
            result = result + jnp.where(step >= k, jump, 0)
    return result


def fold(values, slots):
    total = values[:, 0:slots]
    for k in range(slots, values.shape[1], slots):
        total = total + values[:, k : k + slots]
    return total


def thermal_rows(energy, rho):
    pressure = (ADIABATIC - 1.0) * energy / rho
    sound = jnp.sqrt(ADIABATIC * (ADIABATIC - 1.0) * energy) * (0.5 * VISC_ALPHA / VISC_BETA)
    dense = rho * (0.5 / VISC_BETA)
    rows = lax.broadcasted_iota(jnp.int32, (8, energy.shape[1]), 0)
    return jnp.where(rows == 0, pressure, jnp.where(rows == 1, sound, jnp.where(rows == 2, dense, 0.0)))


def pairs_between(own, columns, size_y):
    result = []
    for near_x, near_y in columns:
        for column, (x, y) in enumerate(own):
            if abs(near_x - x) <= 1 and abs(near_y - y) <= 1:
                result.append((column, near_x * size_y + near_y))
    return sorted(result)


def split_own(own, size_y):
    pairs = pairs_between(own, own, size_y)
    return pairs[::2], pairs[1::2]


def wide(ref, units, row):
    return jnp.concatenate([ref[unit, row : row + 1, :] for unit in units], axis=1)


def multiply(left, right_ref, units):
    right = jnp.concatenate([right_ref[unit] for unit in units], axis=1)
    return jnp.dot(left, right, preferred_element_type=jnp.float32)


def add_forces(column, units, count, span, near_row_ref, warm_row_ref, mine_ref, pair_ref, sums_ref):
    slots = near_row_ref.shape[2]
    mass = wide(near_row_ref, units, 6)
    spots = [wide(near_row_ref, units, f) for f in range(3)]
    near_pressure, near_sound, near_dense = (wide(warm_row_ref, units, k) for k in range(3))
    for first in range(0, count, CHUNK):
        at = slice(first, first + CHUNK)
        dist, approach = pair_ref[at, :], pair_ref[span + first : span + first + CHUNK, :]
        pressure, sound, dense = (
            jnp.concatenate([mine_ref[column, k, at, :]] * len(units), axis=1) for k in range(3)
        )
        safe = jnp.minimum(jnp.maximum(dist, TINY), 1.0)
        inverse = lax.rsqrt(safe)
        half = safe * inverse
        slope = jnp.minimum(inverse, 2.0) + jnp.maximum(half - 2.0, -3.0 * half)
        mu = jnp.minimum(approach, 0.0) / (dist + 0.25 * SOFTENING)
        own_push = mu * (mu - (sound + near_sound)) / (dense + near_dense) + pressure
        weight = mass * slope
        push = weight * (own_push + near_pressure)
        heat = weight * (own_push + pressure) * approach
        terms = [push] + [push * spot for spot in spots] + [heat]
        for k, term in enumerate(terms):
            sums_ref[column, k, at, :] = sums_ref[column, k, at, :] + fold(term, slots)


def sph_kernel(
    size_gx, size_gy, offsets_hbm, velocity_hbm, mass_hbm, energy_hbm, counts_hbm,
    left_ref, right_ref, near_row_ref, warm_row_ref, mine_ref, sums_ref, safe_ref,
    offsets_ref, velocity_ref, mass_ref, energy_ref, counts_ref, own_ref, ext_ref, near_ref, total_ref, dist_ref, pair_ref,
    send_sem, recv_sem, rho_send, rho_recv, in_sem,
):
    count_x, count_y, layers, _, slots = own_ref.shape
    size_y = count_y + 2
    span = layers * slots
    own = [(x, y) for x in range(1, count_x + 1) for y in range(1, count_y + 1)]
    my_x, my_y = lax.axis_index("gx"), lax.axis_index("gy")
    barrier = pltpu.get_barrier_semaphore()
    peers = []
    for dx, dy in DIRECTIONS:
        peers.append(
            (lax.rem(my_x + dx + size_gx, size_gx), lax.rem(my_y + dy + size_gy, size_gy))
        )
    for peer in peers:
        pl.semaphore_signal(barrier, inc=1, device_id=peer, device_id_type=MESH)
    sources = (offsets_hbm, velocity_hbm, mass_hbm, energy_hbm, counts_hbm)
    targets = (offsets_ref, velocity_ref, mass_ref, energy_ref, counts_ref)
    loads = [pltpu.make_async_copy(a, b, in_sem.at[k]) for k, (a, b) in enumerate(zip(sources, targets))]
    for load in loads:
        load.start()
    for load in loads:
        load.wait()
    lane = lax.broadcasted_iota(jnp.int32, (1, slots), 1)
    lanes8 = lax.broadcasted_iota(jnp.int32, (8, slots), 1)
    rows8 = lax.broadcasted_iota(jnp.int32, (8, slots), 0)
    for x in range(count_x):
        for y in range(count_y):
            for z in range(layers):
                at = slice(z, z + 1)
                for f in range(3):
                    height = float(z) if f == 2 else 0.0
                    own_ref[x, y, z, f : f + 1, :] = offsets_ref[f, x, y, at, :] + height
                    own_ref[x, y, z, 3 + f : 4 + f, :] = velocity_ref[f, x, y, at, :]
                own_ref[x, y, z, 6:7, :] = jnp.where(
                    lane < counts_ref[x, y, z], mass_ref[x, y, at, :], 0.0
                )
                own_ref[x, y, z, 7:8, :] = energy_ref[x, y, at, :]
            below = counts_ref[x, y, 0]
            moved = own_ref[x, y, 1]
            step = 1
            while step < slots:
                moved = jnp.where(jnp.bitwise_and(below, step) > 0, pltpu.roll(moved, step, 1), moved)
                step *= 2
            under = lanes8 < below
            own_ref[x, y, 0] = jnp.where(under, own_ref[x, y, 0], moved)
            own_ref[x, y, 1] = jnp.where(jnp.logical_or(under, rows8 != 6), moved, 0.0)

    rows = lax.broadcasted_iota(jnp.int32, (8, slots), 0)
    none = jnp.zeros((8, slots), jnp.float32)
    inner_x, inner_y = range(1, count_x + 1), range(1, count_y + 1)
    low_first = my_y > 1
    side = jnp.where(low_first, 0, count_y + 1)
    other_side = jnp.where(low_first, count_y + 1, 0)

    def place(cell, x, y):
        middle_y = jnp.asarray(y, jnp.float32) - (1.0 + 0.5 * count_y)
        shift = jnp.where(
            rows == 0, float(x - 1) - 0.5 * count_x, jnp.where(rows == 1, middle_y, -0.5 * layers)
        )
        placed = jnp.where(rows < 3, (cell + shift) * (1.0 / SMOOTHING), cell)
        other = pltpu.roll(placed, 5, 0)
        length = jnp.sum(jnp.where(rows < 3, placed * placed, 0.0), axis=0, keepdims=True)
        moving = jnp.sum(jnp.where(rows < 3, placed * other, 0.0), axis=0, keepdims=True)
        return placed, other, length, moving

    def enter(placed, length, moving, x, y, z):
        unit = (x * size_y + y) * layers + z
        features = jnp.where(rows < 6, placed, jnp.where(rows == 6, length, moving))
        high, middle, low = split(features)
        ones = jnp.where(rows < 3, 1.0, 0.0)
        tile = jnp.concatenate([high, high, high, middle, middle, low, ones, none], axis=0)
        right_ref[unit] = tile.astype(jnp.bfloat16)
        near_row_ref[unit] = placed

    def enter_near(x, y, z):
        placed, _, length, moving = place(ext_ref[x, y, z], x, y)
        enter(placed, length, moving, x, y, z)

    def coefficients(terms, constant):
        high, middle, low = split(terms)
        parts = split(constant)
        last = jnp.where(
            rows == 0, parts[0], jnp.where(rows == 1, parts[1], jnp.where(rows == 2, parts[2], 0.0))
        )
        tile = jnp.concatenate([high, middle, low, high, middle, high, last, none], axis=0)
        return tile.T.astype(jnp.bfloat16)

    def units_of(block):
        return [block * layers + z for z in range(layers)]

    def products(column, block, count):
        return multiply(left_ref[column, 0:count, 0:DEPTH], right_ref, units_of(block))

    def sweep(pairs, count, held_ref, process):
        tables = pairs if isinstance(pairs, tuple) else (pairs,)
        length = len(tables[0])

        def at(step):
            found = [tuple(look_up(step, [pair[k] for pair in table]) for k in range(2)) for table in tables]
            if len(found) == 1:
                return found[0]
            return tuple(jnp.where(low_first, a, b) for a, b in zip(*found))

        def step_zero(step):
            found = [table[min(step, length - 1)] for table in tables]
            if len(found) == 1:
                return tuple(jnp.int32(value) for value in found[0])
            return tuple(jnp.where(low_first, a, b) for a, b in zip(*found))

        start = step_zero(0) + step_zero(1)
        held_ref[...] = products(start[0], start[1], count)

        def body(step, carry):
            column, block, next_column, next_block = carry
            following = products(next_column, next_block, count)
            process(column, block)
            held_ref[...] = following
            return (next_column, next_block) + at(jnp.minimum(step + 2, length - 1))

        lax.fori_loop(0, length, body, start, unroll=(length if length <= 8 else 4) if count == span else 2)

    def density_step(column, block):
        mass = wide(near_row_ref, units_of(block), 6)
        for first in range(0, span, CHUNK):
            at = slice(first, first + CHUNK)
            dist = jnp.maximum(dist_ref[at, :], TINY)
            outer = jnp.maximum(1.0 - dist * lax.rsqrt(dist), 0.0)
            kernel = jnp.where(dist < 0.25, 0.5 - 3.0 * (dist * outer), outer * outer * outer)
            total_ref[column, at, :] = total_ref[column, at, :] + fold(kernel * mass, slots)

    def force_step(column, block):
        add_forces(
            column, units_of(block), span, span, near_row_ref, warm_row_ref, mine_ref, pair_ref, sums_ref
        )

    across = [(x, y) for x in (0, count_x + 1) for y in inner_y]
    low_side = [(x, 0) for x in range(count_x + 2)]
    high_side = [(x, count_y + 1) for x in range(count_x + 2)]

    def wait_side(which, copies):
        for copy, (_, dy) in zip(copies, DIRECTIONS):
            if dy == which:
                copy.wait_recv()

    def block_of(x, y):
        return x * size_y + y

    def pairs_with(columns):
        return pairs_between(own, columns, size_y)

    def start_own():
        for column, (x, y) in enumerate(own):
            for z in range(layers):
                placed, other, length, moving = place(own_ref[x - 1, y - 1, z], x, y)
                enter(placed, length, moving, x, y, z)
                gap = jnp.where(rows < 3, -0.5 * placed, jnp.where(rows == 6, 0.25, 0.0))
                left_ref[column, pl.ds(z * slots, slots), 0:DEPTH] = coefficients(gap, 0.25 * length)
                swapped = jnp.where(rows < 3, other, pltpu.roll(placed, 3, 0))
                rate = jnp.where(rows < 6, -0.25 * swapped, jnp.where(rows == 7, 0.25, 0.0))
                left_ref[column, pl.ds(span + z * slots, slots), 0:DEPTH] = coefficients(rate, 0.25 * moving)
        total_ref[...] = jnp.zeros_like(total_ref)
        spare = right_ref.shape[0] - 1
        right_ref[spare] = jnp.zeros(right_ref.shape[1:], jnp.bfloat16)
        near_row_ref[spare] = none
        warm_row_ref[spare] = none + 1.0
        sums_ref[...] = jnp.zeros_like(sums_ref)
        sweep(pairs_with(own), span, dist_ref, density_step)

    first_rows = my_y < 2
    pl.when(first_rows)(start_own)
    pl.semaphore_wait(barrier, len(peers))
    copies = make_copies(peers, own_ref, ext_ref, count_x, count_y, send_sem, recv_sem)
    for copy in copies:
        copy.start()
    pl.when(jnp.logical_not(first_rows))(start_own)

    pl.when(low_first)(lambda: wait_side(1, copies))
    pl.when(jnp.logical_not(low_first))(lambda: wait_side(-1, copies))
    for x in range(count_x + 2):
        for z in range(layers):
            enter_near(x, side, z)
    sweep((pairs_with(low_side), pairs_with(high_side)), span, dist_ref, density_step)
    wait_side(0, copies)
    for x, y in across:
        for z in range(layers):
            enter_near(x, y, z)
    sweep(pairs_with(across), span, dist_ref, density_step)
    in_order = [jnp.where(low_first, 1 + k, count_y - k) for k in range(count_y)]
    early = count_y > 1
    rho_copies = make_copies(peers, safe_ref, near_ref, count_x, count_y, rho_send, rho_recv)

    def start_side(which):
        for copy, (_, dy) in zip(rho_copies, DIRECTIONS):
            if dy == which:
                copy.start()

    def start_first():
        pl.when(low_first)(lambda: start_side(-1))
        pl.when(jnp.logical_not(low_first))(lambda: start_side(1))

    def finish_density(y):
        for x in inner_x:
            for z in range(layers):
                total = total_ref[(x - 1) * count_y + y - 1, z * slots : (z + 1) * slots, :].T
                row = jnp.sum(total, axis=0, keepdims=True) * (2.0 * NORMALISE)
                held = own_ref[x - 1, y - 1, z, 6:7, :] > 0.0
                safe_ref[x - 1, y - 1, z : z + 1, :] = jnp.where(held, row, 1.0)

    if early:
        finish_density(in_order[0])
        start_first()
    pl.when(low_first)(lambda: wait_side(-1, copies))
    pl.when(jnp.logical_not(low_first))(lambda: wait_side(1, copies))
    for x in range(count_x + 2):
        for z in range(layers):
            enter_near(x, other_side, z)
    sweep((pairs_with(high_side), pairs_with(low_side)), span, dist_ref, density_step)
    for y in in_order[1:] if early else in_order:
        finish_density(y)
    if not early:
        start_first()
    start_side(0)
    pl.when(low_first)(lambda: start_side(1))
    pl.when(jnp.logical_not(low_first))(lambda: start_side(-1))
    for copy in copies:
        copy.wait_send()
    for column, (x, y) in enumerate(own):
        for z in range(layers):
            warm = thermal_rows(own_ref[x - 1, y - 1, z, 7:8, :], safe_ref[x - 1, y - 1, z : z + 1, :])
            warm_row_ref[block_of(x, y) * layers + z] = warm
            turned = jnp.concatenate([warm] + [none] * 7, axis=0).T
            for k in range(3):
                mine_ref[column, k, pl.ds(z * slots, slots), :] = jnp.broadcast_to(
                    turned[:, k : k + 1], (slots, slots)
                )
    sweep(split_own(own, size_y)[0], 2 * span, pair_ref, force_step)
    for copy in rho_copies:
        copy.wait()
    halo = across + low_side + high_side
    for x, y in halo:
        for z in range(layers):
            warm = thermal_rows(ext_ref[x, y, z, 7:8, :], near_ref[x, y, z : z + 1, :])
            warm_row_ref[block_of(x, y) * layers + z] = warm


def force_kernel(
    shape, counts_hbm, left_ref, right_ref, near_row_ref, warm_row_ref, mine_ref, start_ref, safe_ref,
    density_out, accel_out, heat_out, counts_ref, sums_ref, pair_ref, table_ref, length_ref, in_sem,
):
    count_x, count_y, layers, slots = shape
    size_y = count_y + 2
    span = layers * slots
    own = [(x, y) for x in range(1, count_x + 1) for y in range(1, count_y + 1)]
    columns = [(x, y) for x in range(count_x + 2) for y in range(size_y)]
    spare = len(columns) * layers
    done = split_own(own, size_y)[0]
    load = pltpu.make_async_copy(counts_hbm, counts_ref, in_sem)
    load.start()
    sums_ref[...] = start_ref[...]
    second = []
    for block in range(len(columns)):
        held = jnp.sum(near_row_ref[block * layers + 1, 6:7, :])
        second.append(jnp.where(held > 0.0, 1, 0))
    for column, (x, y) in enumerate(own):
        length = jnp.int32(0)
        for pair in pairs_between([(x, y)], columns, size_y):
            if (column, pair[1]) not in done:
                table_ref[column, length] = pair[1] * layers
                table_ref[column, length + 1] = pair[1] * layers + 1
                length = length + 1 + second[pair[1]]
        for k in range(2 * UNITS):
            table_ref[column, length + k] = spare
        length_ref[column] = length

    load.wait()

    def run(column, count):
        def products(units):
            left = [left_ref[column, first : first + count, 0:DEPTH] for first in (0, span)]
            return multiply(jnp.concatenate(left, axis=0), right_ref, units)

        def keep(found):
            pair_ref[0:count, :] = found[0:count]
            pair_ref[span : span + count, :] = found[count:]

        def units_at(step):
            return tuple(table_ref[column, step * UNITS + k] for k in range(UNITS))

        keep(products(units_at(0)))

        def body(step, carry):
            units, following = carry
            found = products(following)
            add_forces(
                column, units, count, span, near_row_ref, warm_row_ref, mine_ref, pair_ref, sums_ref
            )
            keep(found)
            return following, units_at(jnp.minimum(step + 2, steps))

        steps = (length_ref[column] + (UNITS - 1)) // UNITS
        lax.fori_loop(0, steps, body, (units_at(0), units_at(1)))

    def each(column, carry):
        x, y = column // count_y, lax.rem(column, count_y)
        held = counts_ref[x, y, 0] + counts_ref[x, y, 1]
        for count in range(CHUNK, span + 1, CHUNK):
            pl.when(jnp.logical_and(held > count - CHUNK, held <= count))(functools.partial(run, column, count))
        return carry

    lax.fori_loop(0, len(own), each, 0)
    factor = 1.5 * NORMALISE / SMOOTHING
    rows = lax.broadcasted_iota(jnp.int32, (8, slots), 0)
    lane = lax.broadcasted_iota(jnp.int32, (8, slots), 1)
    for column, (x, y) in enumerate(own):
        packed = []
        for z in range(layers):
            at = slice(z * slots, (z + 1) * slots)
            sums = [jnp.sum(sums_ref[column, k, at, :].T, axis=0, keepdims=True) for k in range(SUMS)]
            unit = (x * size_y + y) * layers + z
            result = jnp.broadcast_to(safe_ref[x - 1, y - 1, z : z + 1, :], (8, slots))
            for f in range(3):
                value = (near_row_ref[unit, f : f + 1, :] * sums[0] - sums[1 + f]) * factor
                result = jnp.where(rows == f, value, result)
            packed.append(jnp.where(rows == 3, sums[4] * (-2.0 * factor), result))
        below = counts_ref[x - 1, y - 1, 0]
        back = jnp.where(below == slots, 0, slots - below)
        lower, upper = pltpu.roll(packed[0], back, 1), pltpu.roll(packed[1], back, 1)
        cells = [packed[0], jnp.where(lane < slots - below, lower, upper)]
        for z in range(layers):
            cell = jnp.where(lane < counts_ref[x - 1, y - 1, z], cells[z], 0.0)
            for f in range(3):
                accel_out[f, x - 1, y - 1, z : z + 1, :] = cell[f : f + 1]
            heat_out[x - 1, y - 1, z : z + 1, :] = cell[3:4]
            density_out[x - 1, y - 1, z : z + 1, :] = cell[4:5]


def shards(offsets, velocity, mass, energy, counts):
    slots = mass.shape[-1]
    count_x, count_y, layers = mass.shape[:3]
    wide_x, wide_y = count_x + 2, count_y + 2
    own = count_x * count_y
    span = layers * slots
    vmem = pl.BlockSpec(memory_space=VMEM)
    units = wide_x * wide_y * layers + 1
    shapes = (mass.shape, (3,) + mass.shape, mass.shape)
    between = [
        VMEM((own, 2 * span, 128), jnp.bfloat16),
        VMEM((units, DEPTH, slots), jnp.bfloat16),
        VMEM((units, 8, slots), jnp.float32),
        VMEM((units, 8, slots), jnp.float32),
        VMEM((own, 3, span, slots), jnp.float32),
        VMEM((own, SUMS, span, slots), jnp.float32),
        VMEM((count_x, count_y, layers, slots), jnp.float32),
    ]
    hbm = pl.BlockSpec(memory_space=pltpu.HBM)
    inputs = [
        pltpu.with_memory_space_constraint(x, pltpu.HBM)
        for x in (offsets, velocity, mass, energy, counts)
    ]
    sems = pltpu.SemaphoreType.DMA((len(DIRECTIONS),))
    cell_shape = (layers, 8, slots)
    results = pl.pallas_call(
        functools.partial(sph_kernel, lax.axis_size("gx"), lax.axis_size("gy")),
        out_shape=between,
        in_specs=[hbm] * 5,
        out_specs=[vmem] * len(between),
        scratch_shapes=[
            VMEM(offsets.shape, jnp.float32),
            VMEM(velocity.shape, jnp.float32),
            VMEM(mass.shape, jnp.float32),
            VMEM(energy.shape, jnp.float32),
            pltpu.SMEM(counts.shape, jnp.int32),
            VMEM((count_x, count_y) + cell_shape, jnp.float32),
            VMEM((wide_x, wide_y) + cell_shape, jnp.float32),
            VMEM((wide_x, wide_y, layers, slots), jnp.float32),
            VMEM((own, span, slots), jnp.float32),
            VMEM((span, span), jnp.float32),
            VMEM((2 * span, span), jnp.float32),
            sems,
            sems,
            sems,
            sems,
            pltpu.SemaphoreType.DMA((5,)),
        ],
        compiler_params=pltpu.CompilerParams(
            collective_id=0, has_side_effects=True, vmem_limit_bytes=VMEM_GRANT
        ),
        name="sph",
    )(*inputs)
    return pl.pallas_call(
        functools.partial(force_kernel, mass.shape),
        out_shape=[jax.ShapeDtypeStruct(shape, jnp.float32) for shape in shapes],
        in_specs=[hbm] + [vmem] * len(between),
        out_specs=[vmem] * 3,
        scratch_shapes=[
            pltpu.SMEM(counts.shape, jnp.int32),
            VMEM((own, SUMS, span, slots), jnp.float32),
            VMEM((2 * span, UNITS * slots), jnp.float32),
            pltpu.SMEM((own, 9 * layers + 2 * UNITS), jnp.int32),
            pltpu.SMEM((own,), jnp.int32),
            pltpu.SemaphoreType.DMA,
        ],
        compiler_params=pltpu.CompilerParams(vmem_limit_bytes=VMEM_GRANT),
        name="force",
    )(inputs[4], *[pltpu.with_memory_space_constraint(result, VMEM) for result in results])


def solution(mesh):
    in_specs = (
        P(None, "gx", "gy", None, None),
        P(None, "gx", "gy", None, None),
        P("gx", "gy", None, None),
        P("gx", "gy", None, None),
        P("gx", "gy", None),
    )
    out_specs = (
        P("gx", "gy", None, None),
        P(None, "gx", "gy", None, None),
        P("gx", "gy", None, None),
    )
    return jax.shard_map(shards, mesh=mesh, in_specs=in_specs, out_specs=out_specs, check_vma=False)
```

```python
import functools
import math

import jax
import jax.numpy as jnp
from jax import lax
from jax.experimental import pallas as pl
from jax.experimental.pallas import tpu as pltpu
from jax.sharding import PartitionSpec as P

SMOOTHING = 0.5
NORMALISE = 1.0 / (math.pi * 0.125)
ADIABATIC = 5.0 / 3.0
VISC_ALPHA = 1.0
VISC_BETA = 2.0
SOFTENING = 0.01
TINY = 1e-30
VMEM = pltpu.VMEM
MESH = pl.DeviceIdType.MESH
DIRECTIONS = [(dx, dy) for dx in (-1, 0, 1) for dy in (-1, 0, 1) if (dx, dy) != (0, 0)]
DEPTH = 64
SUMS = 5
VMEM_GRANT = 16 * 2**20
CHUNK = 32
UNITS = 3


def edge(step, count):
    if step == 0:
        return (0, 1, count)
    if step == 1:
        return (count - 1, 0, 1)
    return (0, count + 1, 1)


def make_copies(peers, own_ref, out_ref, count_x, count_y, send_sem, recv_sem):
    copies = []
    for k, (dx, dy) in enumerate(DIRECTIONS):
        from_x, to_x, width_x = edge(dx, count_x)
        from_y, to_y, width_y = edge(dy, count_y)
        copy = pltpu.make_async_remote_copy(
            src_ref=own_ref.at[pl.ds(from_x, width_x), pl.ds(from_y, width_y)],
            dst_ref=out_ref.at[pl.ds(to_x, width_x), pl.ds(to_y, width_y)],
            send_sem=send_sem.at[k],
            recv_sem=recv_sem.at[k],
            device_id=peers[k],
            device_id_type=MESH,
        )
        copies.append(copy)
    return copies


def split(values):
    high = values.astype(jnp.bfloat16).astype(jnp.float32)
    rest = values - high
    middle = rest.astype(jnp.bfloat16).astype(jnp.float32)
    return high, middle, rest - middle


def look_up(step, values):
    result = step + values[0]
    for k in range(1, len(values)):
        jump = values[k] - values[k - 1] - 1
        if jump:
            result = result + jnp.where(step >= k, jump, 0)
    return result


def fold(values, slots):
    total = values[:, 0:slots]
    for k in range(slots, values.shape[1], slots):
        total = total + values[:, k : k + slots]
    return total


def thermal_rows(energy, rho):
    pressure = (ADIABATIC - 1.0) * energy / rho
    sound = jnp.sqrt(ADIABATIC * (ADIABATIC - 1.0) * energy) * (0.5 * VISC_ALPHA / VISC_BETA)
    dense = rho * (0.5 / VISC_BETA)
    rows = lax.broadcasted_iota(jnp.int32, (8, energy.shape[1]), 0)
    return jnp.where(rows == 0, pressure, jnp.where(rows == 1, sound, jnp.where(rows == 2, dense, 0.0)))


def pairs_between(own, columns, size_y):
    result = []
    for near_x, near_y in columns:
        for column, (x, y) in enumerate(own):
            if abs(near_x - x) <= 1 and abs(near_y - y) <= 1:
                result.append((column, near_x * size_y + near_y))
    return sorted(result)


def split_own(own, size_y):
    pairs = pairs_between(own, own, size_y)
    return pairs[::2], pairs[1::4], pairs[3::4]


def wide(ref, units, row):
    return jnp.concatenate([ref[unit, row : row + 1, :] for unit in units], axis=1)


def multiply(left, right_ref, units):
    right = jnp.concatenate([right_ref[unit] for unit in units], axis=1)
    return jnp.dot(left, right, preferred_element_type=jnp.float32)


def add_forces(column, units, count, span, near_row_ref, warm_row_ref, mine_ref, pair_ref, sums_ref):
    slots = near_row_ref.shape[2]
    mass = wide(near_row_ref, units, 6)
    spots = [wide(near_row_ref, units, f) for f in range(3)]
    near_pressure, near_sound, near_dense = (wide(warm_row_ref, units, k) for k in range(3))
    for first in range(0, count, CHUNK):
        at = slice(first, first + CHUNK)
        dist, approach = pair_ref[at, :], pair_ref[span + first : span + first + CHUNK, :]
        pressure, sound, dense = (
            jnp.concatenate([mine_ref[column, k, at, :]] * len(units), axis=1) for k in range(3)
        )
        safe = jnp.minimum(jnp.maximum(dist, TINY), 1.0)
        inverse = lax.rsqrt(safe)
        half = safe * inverse
        slope = jnp.minimum(inverse, 2.0) + jnp.maximum(half - 2.0, -3.0 * half)
        mu = jnp.minimum(approach, 0.0) / (dist + 0.25 * SOFTENING)
        own_push = mu * (mu - (sound + near_sound)) / (dense + near_dense) + pressure
        weight = mass * slope
        push = weight * (own_push + near_pressure)
        heat = weight * (own_push + pressure) * approach
        terms = [push] + [push * spot for spot in spots] + [heat]
        for k, term in enumerate(terms):
            sums_ref[column, k, at, :] = sums_ref[column, k, at, :] + fold(term, slots)


def sph_kernel(
    size_gx, size_gy, offsets_hbm, velocity_hbm, mass_hbm, energy_hbm, counts_hbm,
    left_ref, right_ref, near_row_ref, warm_row_ref, mine_ref, sums_ref, safe_ref,
    offsets_ref, velocity_ref, mass_ref, energy_ref, counts_ref, own_ref, ext_ref, near_ref, total_ref, dist_ref, pair_ref,
    send_sem, recv_sem, rho_send, rho_recv, in_sem,
):
    count_x, count_y, layers, _, slots = own_ref.shape
    size_y = count_y + 2
    span = layers * slots
    own = [(x, y) for x in range(1, count_x + 1) for y in range(1, count_y + 1)]
    my_x, my_y = lax.axis_index("gx"), lax.axis_index("gy")
    barrier = pltpu.get_barrier_semaphore()
    peers = []
    for dx, dy in DIRECTIONS:
        peers.append(
            (lax.rem(my_x + dx + size_gx, size_gx), lax.rem(my_y + dy + size_gy, size_gy))
        )
    for peer in peers:
        pl.semaphore_signal(barrier, inc=1, device_id=peer, device_id_type=MESH)
    sources = (offsets_hbm, velocity_hbm, mass_hbm, energy_hbm, counts_hbm)
    targets = (offsets_ref, velocity_ref, mass_ref, energy_ref, counts_ref)
    loads = [pltpu.make_async_copy(a, b, in_sem.at[k]) for k, (a, b) in enumerate(zip(sources, targets))]
    for load in loads:
        load.start()
    for load in loads:
        load.wait()
    lane = lax.broadcasted_iota(jnp.int32, (1, slots), 1)
    lanes8 = lax.broadcasted_iota(jnp.int32, (8, slots), 1)
    rows8 = lax.broadcasted_iota(jnp.int32, (8, slots), 0)
    for x in range(count_x):
        for y in range(count_y):
            for z in range(layers):
                at = slice(z, z + 1)
                for f in range(3):
                    height = float(z) if f == 2 else 0.0
                    own_ref[x, y, z, f : f + 1, :] = offsets_ref[f, x, y, at, :] + height
                    own_ref[x, y, z, 3 + f : 4 + f, :] = velocity_ref[f, x, y, at, :]
                own_ref[x, y, z, 6:7, :] = jnp.where(
                    lane < counts_ref[x, y, z], mass_ref[x, y, at, :], 0.0
                )
                own_ref[x, y, z, 7:8, :] = energy_ref[x, y, at, :]
            below = counts_ref[x, y, 0]
            moved = own_ref[x, y, 1]
            step = 1
            while step < slots:
                moved = jnp.where(jnp.bitwise_and(below, step) > 0, pltpu.roll(moved, step, 1), moved)
                step *= 2
            under = lanes8 < below
            own_ref[x, y, 0] = jnp.where(under, own_ref[x, y, 0], moved)
            own_ref[x, y, 1] = jnp.where(jnp.logical_or(under, rows8 != 6), moved, 0.0)

    rows = lax.broadcasted_iota(jnp.int32, (8, slots), 0)
    none = jnp.zeros((8, slots), jnp.float32)
    inner_x, inner_y = range(1, count_x + 1), range(1, count_y + 1)
    low_first = my_y > 1
    side = jnp.where(low_first, 0, count_y + 1)
    other_side = jnp.where(low_first, count_y + 1, 0)

    def place(cell, x, y):
        middle_y = jnp.asarray(y, jnp.float32) - (1.0 + 0.5 * count_y)
        shift = jnp.where(
            rows == 0, float(x - 1) - 0.5 * count_x, jnp.where(rows == 1, middle_y, -0.5 * layers)
        )
        placed = jnp.where(rows < 3, (cell + shift) * (1.0 / SMOOTHING), cell)
        other = pltpu.roll(placed, 5, 0)
        length = jnp.sum(jnp.where(rows < 3, placed * placed, 0.0), axis=0, keepdims=True)
        moving = jnp.sum(jnp.where(rows < 3, placed * other, 0.0), axis=0, keepdims=True)
        return placed, other, length, moving

    def enter(placed, length, moving, x, y, z):
        unit = (x * size_y + y) * layers + z
        features = jnp.where(rows < 6, placed, jnp.where(rows == 6, length, moving))
        high, middle, low = split(features)
        ones = jnp.where(rows < 3, 1.0, 0.0)
        tile = jnp.concatenate([high, high, high, middle, middle, low, ones, none], axis=0)
        right_ref[unit] = tile.astype(jnp.bfloat16)
        near_row_ref[unit] = placed

    def enter_near(x, y, z):
        placed, _, length, moving = place(ext_ref[x, y, z], x, y)
        enter(placed, length, moving, x, y, z)

    def coefficients(terms, constant):
        high, middle, low = split(terms)
        parts = split(constant)
        last = jnp.where(
            rows == 0, parts[0], jnp.where(rows == 1, parts[1], jnp.where(rows == 2, parts[2], 0.0))
        )
        tile = jnp.concatenate([high, middle, low, high, middle, high, last, none], axis=0)
        return tile.T.astype(jnp.bfloat16)

    def units_of(block):
        return [block * layers + z for z in range(layers)]

    def products(column, block, count):
        return multiply(left_ref[column, 0:count, 0:DEPTH], right_ref, units_of(block))

    def sweep(pairs, count, held_ref, process):
        tables = pairs if isinstance(pairs, tuple) else (pairs,)
        length = len(tables[0])

        def at(step):
            found = [tuple(look_up(step, [pair[k] for pair in table]) for k in range(2)) for table in tables]
            if len(found) == 1:
                return found[0]
            return tuple(jnp.where(low_first, a, b) for a, b in zip(*found))

        def step_zero(step):
            found = [table[min(step, length - 1)] for table in tables]
            if len(found) == 1:
                return tuple(jnp.int32(value) for value in found[0])
            return tuple(jnp.where(low_first, a, b) for a, b in zip(*found))

        start = step_zero(0) + step_zero(1)
        held_ref[...] = products(start[0], start[1], count)

        def body(step, carry):
            column, block, next_column, next_block = carry
            following = products(next_column, next_block, count)
            process(column, block)
            held_ref[...] = following
            return (next_column, next_block) + at(jnp.minimum(step + 2, length - 1))

        lax.fori_loop(0, length, body, start, unroll=length)

    def density_step(column, block):
        mass = wide(near_row_ref, units_of(block), 6)
        for first in range(0, span, CHUNK):
            at = slice(first, first + CHUNK)
            dist = jnp.maximum(dist_ref[at, :], TINY)
            outer = jnp.maximum(1.0 - dist * lax.rsqrt(dist), 0.0)
            kernel = jnp.where(dist < 0.25, 0.5 - 3.0 * (dist * outer), outer * outer * outer)
            total_ref[column, at, :] = total_ref[column, at, :] + fold(kernel * mass, slots)

    def force_step(column, block):
        add_forces(
            column, units_of(block), span, span, near_row_ref, warm_row_ref, mine_ref, pair_ref, sums_ref
        )

    across = [(x, y) for x in (0, count_x + 1) for y in inner_y]
    low_side = [(x, 0) for x in range(count_x + 2)]
    high_side = [(x, count_y + 1) for x in range(count_x + 2)]

    def wait_side(which, copies):
        for copy, (_, dy) in zip(copies, DIRECTIONS):
            if dy == which:
                copy.wait_recv()

    def block_of(x, y):
        return x * size_y + y

    def pairs_with(columns):
        return pairs_between(own, columns, size_y)

    def start_own():
        for column, (x, y) in enumerate(own):
            for z in range(layers):
                placed, other, length, moving = place(own_ref[x - 1, y - 1, z], x, y)
                enter(placed, length, moving, x, y, z)
                gap = jnp.where(rows < 3, -0.5 * placed, jnp.where(rows == 6, 0.25, 0.0))
                left_ref[column, pl.ds(z * slots, slots), 0:DEPTH] = coefficients(gap, 0.25 * length)
                swapped = jnp.where(rows < 3, other, pltpu.roll(placed, 3, 0))
                rate = jnp.where(rows < 6, -0.25 * swapped, jnp.where(rows == 7, 0.25, 0.0))
                left_ref[column, pl.ds(span + z * slots, slots), 0:DEPTH] = coefficients(rate, 0.25 * moving)
        total_ref[...] = jnp.zeros_like(total_ref)
        spare = right_ref.shape[0] - 1
        right_ref[spare] = jnp.zeros(right_ref.shape[1:], jnp.bfloat16)
        near_row_ref[spare] = none
        warm_row_ref[spare] = none + 1.0
        sums_ref[...] = jnp.zeros_like(sums_ref)
        sweep(pairs_with(own), span, dist_ref, density_step)

    first_rows = my_y < 2
    pl.when(first_rows)(start_own)
    pl.semaphore_wait(barrier, len(peers))
    copies = make_copies(peers, own_ref, ext_ref, count_x, count_y, send_sem, recv_sem)
    for copy in copies:
        copy.start()
    pl.when(jnp.logical_not(first_rows))(start_own)

    pl.when(low_first)(lambda: wait_side(1, copies))
    pl.when(jnp.logical_not(low_first))(lambda: wait_side(-1, copies))
    for x in range(count_x + 2):
        for z in range(layers):
            enter_near(x, side, z)
    sweep((pairs_with(low_side), pairs_with(high_side)), span, dist_ref, density_step)
    wait_side(0, copies)
    for x, y in across:
        for z in range(layers):
            enter_near(x, y, z)
    sweep(pairs_with(across), span, dist_ref, density_step)
    in_order = [jnp.where(low_first, 1 + k, count_y - k) for k in range(count_y)]
    early = count_y > 1
    rho_copies = make_copies(peers, safe_ref, near_ref, count_x, count_y, rho_send, rho_recv)

    def start_side(which):
        for copy, (_, dy) in zip(rho_copies, DIRECTIONS):
            if dy == which:
                copy.start()

    def start_first():
        pl.when(low_first)(lambda: start_side(-1))
        pl.when(jnp.logical_not(low_first))(lambda: start_side(1))

    def finish_density(y):
        for x in inner_x:
            for z in range(layers):
                total = total_ref[(x - 1) * count_y + y - 1, z * slots : (z + 1) * slots, :].T
                row = jnp.sum(total, axis=0, keepdims=True) * (2.0 * NORMALISE)
                held = own_ref[x - 1, y - 1, z, 6:7, :] > 0.0
                safe_ref[x - 1, y - 1, z : z + 1, :] = jnp.where(held, row, 1.0)

    if early:
        finish_density(in_order[0])
        start_first()
    pl.when(low_first)(lambda: wait_side(-1, copies))
    pl.when(jnp.logical_not(low_first))(lambda: wait_side(1, copies))
    for x in range(count_x + 2):
        for z in range(layers):
            enter_near(x, other_side, z)
    sweep((pairs_with(high_side), pairs_with(low_side)), span, dist_ref, density_step)
    for y in in_order[1:] if early else in_order:
        finish_density(y)
    if not early:
        start_first()
    start_side(0)
    pl.when(low_first)(lambda: start_side(1))
    pl.when(jnp.logical_not(low_first))(lambda: start_side(-1))
    for copy in copies:
        copy.wait_send()
    for column, (x, y) in enumerate(own):
        for z in range(layers):
            warm = thermal_rows(own_ref[x - 1, y - 1, z, 7:8, :], safe_ref[x - 1, y - 1, z : z + 1, :])
            warm_row_ref[block_of(x, y) * layers + z] = warm
            turned = jnp.concatenate([warm] + [none] * 7, axis=0).T
            for k in range(3):
                mine_ref[column, k, pl.ds(z * slots, slots), :] = jnp.broadcast_to(
                    turned[:, k : k + 1], (slots, slots)
                )
    always, waiting, _ = split_own(own, size_y)
    sweep(always, 2 * span, pair_ref, force_step)
    if waiting:
        pl.when(my_y == 0)(lambda: sweep(waiting, 2 * span, pair_ref, force_step))
    for copy in rho_copies:
        copy.wait()
    halo = across + low_side + high_side
    for x, y in halo:
        for z in range(layers):
            warm = thermal_rows(ext_ref[x, y, z, 7:8, :], near_ref[x, y, z : z + 1, :])
            warm_row_ref[block_of(x, y) * layers + z] = warm


def force_kernel(
    shape, counts_hbm, left_ref, right_ref, near_row_ref, warm_row_ref, mine_ref, start_ref, safe_ref,
    density_out, accel_out, heat_out, counts_ref, sums_ref, pair_ref, table_ref, length_ref, in_sem,
):
    count_x, count_y, layers, slots = shape
    size_y = count_y + 2
    span = layers * slots
    own = [(x, y) for x in range(1, count_x + 1) for y in range(1, count_y + 1)]
    columns = [(x, y) for x in range(count_x + 2) for y in range(size_y)]
    spare = len(columns) * layers
    always, waiting, _ = split_own(own, size_y)
    elsewhere = jnp.where(lax.axis_index("gy") == 0, 0, 1)
    load = pltpu.make_async_copy(counts_hbm, counts_ref, in_sem)
    load.start()
    sums_ref[...] = start_ref[...]
    second = []
    for block in range(len(columns)):
        held = jnp.sum(near_row_ref[block * layers + 1, 6:7, :])
        second.append(jnp.where(held > 0.0, 1, 0))
    for column, (x, y) in enumerate(own):
        length = jnp.int32(0)
        for pair in pairs_between([(x, y)], columns, size_y):
            if (column, pair[1]) not in always:
                table_ref[column, length] = pair[1] * layers
                table_ref[column, length + 1] = pair[1] * layers + 1
                found = 1 + second[pair[1]]
                length = length + (found * elsewhere if (column, pair[1]) in waiting else found)
        for k in range(2 * UNITS):
            table_ref[column, length + k] = spare
        length_ref[column] = length

    load.wait()

    def run(column, count):
        def products(units):
            left = [left_ref[column, first : first + count, 0:DEPTH] for first in (0, span)]
            return multiply(jnp.concatenate(left, axis=0), right_ref, units)

        def keep(found):
            pair_ref[0:count, :] = found[0:count]
            pair_ref[span : span + count, :] = found[count:]

        def units_at(step):
            return tuple(table_ref[column, step * UNITS + k] for k in range(UNITS))

        keep(products(units_at(0)))

        def body(step, carry):
            units, following = carry
            found = products(following)
            add_forces(
                column, units, count, span, near_row_ref, warm_row_ref, mine_ref, pair_ref, sums_ref
            )
            keep(found)
            return following, units_at(jnp.minimum(step + 2, steps))

        steps = (length_ref[column] + (UNITS - 1)) // UNITS
        lax.fori_loop(0, steps, body, (units_at(0), units_at(1)))

    def each(column, carry):
        x, y = column // count_y, lax.rem(column, count_y)
        held = counts_ref[x, y, 0] + counts_ref[x, y, 1]
        for count in range(CHUNK, span + 1, CHUNK):
            pl.when(jnp.logical_and(held > count - CHUNK, held <= count))(functools.partial(run, column, count))
        return carry

    lax.fori_loop(0, len(own), each, 0)
    factor = 1.5 * NORMALISE / SMOOTHING
    rows = lax.broadcasted_iota(jnp.int32, (8, slots), 0)
    lane = lax.broadcasted_iota(jnp.int32, (8, slots), 1)
    for column, (x, y) in enumerate(own):
        packed = []
        for z in range(layers):
            at = slice(z * slots, (z + 1) * slots)
            sums = [jnp.sum(sums_ref[column, k, at, :].T, axis=0, keepdims=True) for k in range(SUMS)]
            unit = (x * size_y + y) * layers + z
            result = jnp.broadcast_to(safe_ref[x - 1, y - 1, z : z + 1, :], (8, slots))
            for f in range(3):
                value = (near_row_ref[unit, f : f + 1, :] * sums[0] - sums[1 + f]) * factor
                result = jnp.where(rows == f, value, result)
            packed.append(jnp.where(rows == 3, sums[4] * (-2.0 * factor), result))
        below = counts_ref[x - 1, y - 1, 0]
        back = jnp.where(below == slots, 0, slots - below)
        lower, upper = pltpu.roll(packed[0], back, 1), pltpu.roll(packed[1], back, 1)
        cells = [packed[0], jnp.where(lane < slots - below, lower, upper)]
        for z in range(layers):
            cell = jnp.where(lane < counts_ref[x - 1, y - 1, z], cells[z], 0.0)
            for f in range(3):
                accel_out[f, x - 1, y - 1, z : z + 1, :] = cell[f : f + 1]
            heat_out[x - 1, y - 1, z : z + 1, :] = cell[3:4]
            density_out[x - 1, y - 1, z : z + 1, :] = cell[4:5]


def shards(offsets, velocity, mass, energy, counts):
    slots = mass.shape[-1]
    count_x, count_y, layers = mass.shape[:3]
    wide_x, wide_y = count_x + 2, count_y + 2
    own = count_x * count_y
    span = layers * slots
    vmem = pl.BlockSpec(memory_space=VMEM)
    units = wide_x * wide_y * layers + 1
    shapes = (mass.shape, (3,) + mass.shape, mass.shape)
    between = [
        VMEM((own, 2 * span, 128), jnp.bfloat16),
        VMEM((units, DEPTH, slots), jnp.bfloat16),
        VMEM((units, 8, slots), jnp.float32),
        VMEM((units, 8, slots), jnp.float32),
        VMEM((own, 3, span, slots), jnp.float32),
        VMEM((own, SUMS, span, slots), jnp.float32),
        VMEM((count_x, count_y, layers, slots), jnp.float32),
    ]
    hbm = pl.BlockSpec(memory_space=pltpu.HBM)
    inputs = [
        pltpu.with_memory_space_constraint(x, pltpu.HBM)
        for x in (offsets, velocity, mass, energy, counts)
    ]
    sems = pltpu.SemaphoreType.DMA((len(DIRECTIONS),))
    cell_shape = (layers, 8, slots)
    results = pl.pallas_call(
        functools.partial(sph_kernel, lax.axis_size("gx"), lax.axis_size("gy")),
        out_shape=between,
        in_specs=[hbm] * 5,
        out_specs=[vmem] * len(between),
        scratch_shapes=[
            VMEM(offsets.shape, jnp.float32),
            VMEM(velocity.shape, jnp.float32),
            VMEM(mass.shape, jnp.float32),
            VMEM(energy.shape, jnp.float32),
            pltpu.SMEM(counts.shape, jnp.int32),
            VMEM((count_x, count_y) + cell_shape, jnp.float32),
            VMEM((wide_x, wide_y) + cell_shape, jnp.float32),
            VMEM((wide_x, wide_y, layers, slots), jnp.float32),
            VMEM((own, span, slots), jnp.float32),
            VMEM((span, span), jnp.float32),
            VMEM((2 * span, span), jnp.float32),
            sems,
            sems,
            sems,
            sems,
            pltpu.SemaphoreType.DMA((5,)),
        ],
        compiler_params=pltpu.CompilerParams(
            collective_id=0, has_side_effects=True, vmem_limit_bytes=VMEM_GRANT
        ),
        name="sph",
    )(*inputs)
    return pl.pallas_call(
        functools.partial(force_kernel, mass.shape),
        out_shape=[jax.ShapeDtypeStruct(shape, jnp.float32) for shape in shapes],
        in_specs=[hbm] + [vmem] * len(between),
        out_specs=[vmem] * 3,
        scratch_shapes=[
            pltpu.SMEM(counts.shape, jnp.int32),
            VMEM((own, SUMS, span, slots), jnp.float32),
            VMEM((2 * span, UNITS * slots), jnp.float32),
            pltpu.SMEM((own, 9 * layers + 2 * UNITS), jnp.int32),
            pltpu.SMEM((own,), jnp.int32),
            pltpu.SemaphoreType.DMA,
        ],
        compiler_params=pltpu.CompilerParams(vmem_limit_bytes=VMEM_GRANT),
        name="force",
    )(inputs[4], *[pltpu.with_memory_space_constraint(result, VMEM) for result in results])


def solution(mesh):
    in_specs = (
        P(None, "gx", "gy", None, None),
        P(None, "gx", "gy", None, None),
        P("gx", "gy", None, None),
        P("gx", "gy", None, None),
        P("gx", "gy", None),
    )
    out_specs = (
        P("gx", "gy", None, None),
        P(None, "gx", "gy", None, None),
        P("gx", "gy", None, None),
    )
    return jax.shard_map(shards, mesh=mesh, in_specs=in_specs, out_specs=out_specs, check_vma=False)
```

```python
import functools
import math

import jax
import jax.numpy as jnp
from jax import lax
from jax.experimental import pallas as pl
from jax.experimental.pallas import tpu as pltpu
from jax.sharding import PartitionSpec as P

SMOOTHING = 0.5
NORMALISE = 1.0 / (math.pi * 0.125)
ADIABATIC = 5.0 / 3.0
VISC_ALPHA = 1.0
VISC_BETA = 2.0
SOFTENING = 0.01
TINY = 1e-30
VMEM = pltpu.VMEM
MESH = pl.DeviceIdType.MESH
DIRECTIONS = [(dx, dy) for dx in (-1, 0, 1) for dy in (-1, 0, 1) if (dx, dy) != (0, 0)]
DEPTH = 64
SUMS = 5
VMEM_GRANT = 16 * 2**20
CHUNK = 32
UNITS = 3


def edge(step, count):
    if step == 0:
        return (0, 1, count)
    if step == 1:
        return (count - 1, 0, 1)
    return (0, count + 1, 1)


def make_copies(peers, own_ref, out_ref, count_x, count_y, send_sem, recv_sem):
    copies = []
    for k, (dx, dy) in enumerate(DIRECTIONS):
        from_x, to_x, width_x = edge(dx, count_x)
        from_y, to_y, width_y = edge(dy, count_y)
        copy = pltpu.make_async_remote_copy(
            src_ref=own_ref.at[pl.ds(from_x, width_x), pl.ds(from_y, width_y)],
            dst_ref=out_ref.at[pl.ds(to_x, width_x), pl.ds(to_y, width_y)],
            send_sem=send_sem.at[k],
            recv_sem=recv_sem.at[k],
            device_id=peers[k],
            device_id_type=MESH,
        )
        copies.append(copy)
    return copies


def split(values):
    high = values.astype(jnp.bfloat16).astype(jnp.float32)
    rest = values - high
    middle = rest.astype(jnp.bfloat16).astype(jnp.float32)
    return high, middle, rest - middle


def look_up(step, values):
    result = step + values[0]
    for k in range(1, len(values)):
        jump = values[k] - values[k - 1] - 1
        if jump:
            result = result + jnp.where(step >= k, jump, 0)
    return result


def fold(values, slots):
    total = values[:, 0:slots]
    for k in range(slots, values.shape[1], slots):
        total = total + values[:, k : k + slots]
    return total


def thermal_rows(energy, rho):
    pressure = (ADIABATIC - 1.0) * energy / rho
    sound = jnp.sqrt(ADIABATIC * (ADIABATIC - 1.0) * energy) * (0.5 * VISC_ALPHA / VISC_BETA)
    dense = rho * (0.5 / VISC_BETA)
    rows = lax.broadcasted_iota(jnp.int32, (8, energy.shape[1]), 0)
    return jnp.where(rows == 0, pressure, jnp.where(rows == 1, sound, jnp.where(rows == 2, dense, 0.0)))


def pairs_between(own, columns, size_y):
    result = []
    for near_x, near_y in columns:
        for column, (x, y) in enumerate(own):
            if abs(near_x - x) <= 1 and abs(near_y - y) <= 1:
                result.append((column, near_x * size_y + near_y))
    return sorted(result)


def split_own(own, size_y):
    pairs = pairs_between(own, own, size_y)
    return pairs[::2], pairs[1::4], pairs[3::4]


def wide(ref, units, row):
    return jnp.concatenate([ref[unit, row : row + 1, :] for unit in units], axis=1)


def multiply(left, right_ref, units):
    right = jnp.concatenate([right_ref[unit] for unit in units], axis=1)
    return jnp.dot(left, right, preferred_element_type=jnp.float32)


def add_forces(column, units, count, span, near_row_ref, warm_row_ref, mine_ref, pair_ref, sums_ref):
    slots = near_row_ref.shape[2]
    mass = wide(near_row_ref, units, 6)
    spots = [wide(near_row_ref, units, f) for f in range(3)]
    near_pressure, near_sound, near_dense = (wide(warm_row_ref, units, k) for k in range(3))
    for first in range(0, count, CHUNK):
        at = slice(first, first + CHUNK)
        dist, approach = pair_ref[at, :], pair_ref[span + first : span + first + CHUNK, :]
        pressure, sound, dense = (
            jnp.concatenate([mine_ref[column, k, at, :]] * len(units), axis=1) for k in range(3)
        )
        safe = jnp.minimum(jnp.maximum(dist, TINY), 1.0)
        inverse = lax.rsqrt(safe)
        half = safe * inverse
        slope = jnp.minimum(inverse, 2.0) + jnp.maximum(half - 2.0, -3.0 * half)
        mu = jnp.minimum(approach, 0.0) / (dist + 0.25 * SOFTENING)
        own_push = mu * (mu - (sound + near_sound)) / (dense + near_dense) + pressure
        weight = mass * slope
        push = weight * (own_push + near_pressure)
        heat = weight * (own_push + pressure) * approach
        terms = [push] + [push * spot for spot in spots] + [heat]
        for k, term in enumerate(terms):
            sums_ref[column, k, at, :] = sums_ref[column, k, at, :] + fold(term, slots)


def sph_kernel(
    size_gx, size_gy, offsets_hbm, velocity_hbm, mass_hbm, energy_hbm, counts_hbm,
    left_ref, right_ref, near_row_ref, warm_row_ref, mine_ref, sums_ref, safe_ref,
    offsets_ref, velocity_ref, mass_ref, energy_ref, counts_ref, own_ref, ext_ref, near_ref, total_ref, dist_ref, pair_ref,
    send_sem, recv_sem, rho_send, rho_recv, in_sem,
):
    count_x, count_y, layers, _, slots = own_ref.shape
    size_y = count_y + 2
    span = layers * slots
    own = [(x, y) for x in range(1, count_x + 1) for y in range(1, count_y + 1)]
    my_x, my_y = lax.axis_index("gx"), lax.axis_index("gy")
    barrier = pltpu.get_barrier_semaphore()
    peers = []
    for dx, dy in DIRECTIONS:
        peers.append(
            (lax.rem(my_x + dx + size_gx, size_gx), lax.rem(my_y + dy + size_gy, size_gy))
        )
    for peer in peers:
        pl.semaphore_signal(barrier, inc=1, device_id=peer, device_id_type=MESH)
    sources = (offsets_hbm, velocity_hbm, mass_hbm, energy_hbm, counts_hbm)
    targets = (offsets_ref, velocity_ref, mass_ref, energy_ref, counts_ref)
    loads = [pltpu.make_async_copy(a, b, in_sem.at[k]) for k, (a, b) in enumerate(zip(sources, targets))]
    for load in loads:
        load.start()
    for load in loads:
        load.wait()
    lane = lax.broadcasted_iota(jnp.int32, (1, slots), 1)
    lanes8 = lax.broadcasted_iota(jnp.int32, (8, slots), 1)
    rows8 = lax.broadcasted_iota(jnp.int32, (8, slots), 0)
    for x in range(count_x):
        for y in range(count_y):
            for z in range(layers):
                at = slice(z, z + 1)
                for f in range(3):
                    height = float(z) if f == 2 else 0.0
                    own_ref[x, y, z, f : f + 1, :] = offsets_ref[f, x, y, at, :] + height
                    own_ref[x, y, z, 3 + f : 4 + f, :] = velocity_ref[f, x, y, at, :]
                own_ref[x, y, z, 6:7, :] = jnp.where(
                    lane < counts_ref[x, y, z], mass_ref[x, y, at, :], 0.0
                )
                own_ref[x, y, z, 7:8, :] = energy_ref[x, y, at, :]
            below = counts_ref[x, y, 0]
            moved = own_ref[x, y, 1]
            step = 1
            while step < slots:
                moved = jnp.where(jnp.bitwise_and(below, step) > 0, pltpu.roll(moved, step, 1), moved)
                step *= 2
            under = lanes8 < below
            own_ref[x, y, 0] = jnp.where(under, own_ref[x, y, 0], moved)
            own_ref[x, y, 1] = jnp.where(jnp.logical_or(under, rows8 != 6), moved, 0.0)

    rows = lax.broadcasted_iota(jnp.int32, (8, slots), 0)
    none = jnp.zeros((8, slots), jnp.float32)
    inner_x, inner_y = range(1, count_x + 1), range(1, count_y + 1)
    low_first = my_y > 1
    side = jnp.where(low_first, 0, count_y + 1)
    other_side = jnp.where(low_first, count_y + 1, 0)

    def place(cell, x, y):
        middle_y = jnp.asarray(y, jnp.float32) - (1.0 + 0.5 * count_y)
        shift = jnp.where(
            rows == 0, float(x - 1) - 0.5 * count_x, jnp.where(rows == 1, middle_y, -0.5 * layers)
        )
        placed = jnp.where(rows < 3, (cell + shift) * (1.0 / SMOOTHING), cell)
        other = pltpu.roll(placed, 5, 0)
        length = jnp.sum(jnp.where(rows < 3, placed * placed, 0.0), axis=0, keepdims=True)
        moving = jnp.sum(jnp.where(rows < 3, placed * other, 0.0), axis=0, keepdims=True)
        return placed, other, length, moving

    def enter(placed, length, moving, x, y, z):
        unit = (x * size_y + y) * layers + z
        features = jnp.where(rows < 6, placed, jnp.where(rows == 6, length, moving))
        high, middle, low = split(features)
        ones = jnp.where(rows < 3, 1.0, 0.0)
        tile = jnp.concatenate([high, high, high, middle, middle, low, ones, none], axis=0)
        right_ref[unit] = tile.astype(jnp.bfloat16)
        near_row_ref[unit] = placed

    def enter_near(x, y, z):
        placed, _, length, moving = place(ext_ref[x, y, z], x, y)
        enter(placed, length, moving, x, y, z)

    def coefficients(terms, constant):
        high, middle, low = split(terms)
        parts = split(constant)
        last = jnp.where(
            rows == 0, parts[0], jnp.where(rows == 1, parts[1], jnp.where(rows == 2, parts[2], 0.0))
        )
        tile = jnp.concatenate([high, middle, low, high, middle, high, last, none], axis=0)
        return tile.T.astype(jnp.bfloat16)

    def units_of(block):
        return [block * layers + z for z in range(layers)]

    def products(column, block, count):
        return multiply(left_ref[column, 0:count, 0:DEPTH], right_ref, units_of(block))

    def sweep(pairs, count, held_ref, process):
        tables = pairs if isinstance(pairs, tuple) else (pairs,)
        length = len(tables[0])

        def at(step):
            found = [tuple(look_up(step, [pair[k] for pair in table]) for k in range(2)) for table in tables]
            if len(found) == 1:
                return found[0]
            return tuple(jnp.where(low_first, a, b) for a, b in zip(*found))

        def step_zero(step):
            found = [table[min(step, length - 1)] for table in tables]
            if len(found) == 1:
                return tuple(jnp.int32(value) for value in found[0])
            return tuple(jnp.where(low_first, a, b) for a, b in zip(*found))

        start = step_zero(0) + step_zero(1)
        held_ref[...] = products(start[0], start[1], count)

        def body(step, carry):
            column, block, next_column, next_block = carry
            following = products(next_column, next_block, count)
            process(column, block)
            held_ref[...] = following
            return (next_column, next_block) + at(jnp.minimum(step + 2, length - 1))

        lax.fori_loop(0, length, body, start, unroll=length)

    def density_step(column, block):
        mass = wide(near_row_ref, units_of(block), 6)
        for first in range(0, span, CHUNK):
            at = slice(first, first + CHUNK)
            dist = jnp.maximum(dist_ref[at, :], TINY)
            outer = jnp.maximum(1.0 - dist * lax.rsqrt(dist), 0.0)
            kernel = jnp.where(dist < 0.25, 0.5 - 3.0 * (dist * outer), outer * outer * outer)
            total_ref[column, at, :] = total_ref[column, at, :] + fold(kernel * mass, slots)

    def force_step(column, block):
        add_forces(
            column, units_of(block), span, span, near_row_ref, warm_row_ref, mine_ref, pair_ref, sums_ref
        )

    across = [(x, y) for x in (0, count_x + 1) for y in inner_y]
    low_side = [(x, 0) for x in range(count_x + 2)]
    high_side = [(x, count_y + 1) for x in range(count_x + 2)]

    def wait_side(which, copies):
        for copy, (_, dy) in zip(copies, DIRECTIONS):
            if dy == which:
                copy.wait_recv()

    def block_of(x, y):
        return x * size_y + y

    def pairs_with(columns):
        return pairs_between(own, columns, size_y)

    def start_own():
        for column, (x, y) in enumerate(own):
            for z in range(layers):
                placed, other, length, moving = place(own_ref[x - 1, y - 1, z], x, y)
                enter(placed, length, moving, x, y, z)
                gap = jnp.where(rows < 3, -0.5 * placed, jnp.where(rows == 6, 0.25, 0.0))
                left_ref[column, pl.ds(z * slots, slots), 0:DEPTH] = coefficients(gap, 0.25 * length)
                swapped = jnp.where(rows < 3, other, pltpu.roll(placed, 3, 0))
                rate = jnp.where(rows < 6, -0.25 * swapped, jnp.where(rows == 7, 0.25, 0.0))
                left_ref[column, pl.ds(span + z * slots, slots), 0:DEPTH] = coefficients(rate, 0.25 * moving)
        total_ref[...] = jnp.zeros_like(total_ref)
        spare = right_ref.shape[0] - 1
        right_ref[spare] = jnp.zeros(right_ref.shape[1:], jnp.bfloat16)
        near_row_ref[spare] = none
        warm_row_ref[spare] = none + 1.0
        sums_ref[...] = jnp.zeros_like(sums_ref)
        sweep(pairs_with(own), span, dist_ref, density_step)

    first_rows = my_y < 2
    pl.when(first_rows)(start_own)
    pl.semaphore_wait(barrier, len(peers))
    copies = make_copies(peers, own_ref, ext_ref, count_x, count_y, send_sem, recv_sem)
    for copy in copies:
        copy.start()
    pl.when(jnp.logical_not(first_rows))(start_own)

    pl.when(low_first)(lambda: wait_side(1, copies))
    pl.when(jnp.logical_not(low_first))(lambda: wait_side(-1, copies))
    for x in range(count_x + 2):
        for z in range(layers):
            enter_near(x, side, z)
    sweep((pairs_with(low_side), pairs_with(high_side)), span, dist_ref, density_step)
    wait_side(0, copies)
    for x, y in across:
        for z in range(layers):
            enter_near(x, y, z)
    sweep(pairs_with(across), span, dist_ref, density_step)
    in_order = [jnp.where(low_first, 1 + k, count_y - k) for k in range(count_y)]
    early = count_y > 1
    rho_copies = make_copies(peers, safe_ref, near_ref, count_x, count_y, rho_send, rho_recv)

    def start_side(which):
        for copy, (_, dy) in zip(rho_copies, DIRECTIONS):
            if dy == which:
                copy.start()

    def start_first():
        pl.when(low_first)(lambda: start_side(-1))
        pl.when(jnp.logical_not(low_first))(lambda: start_side(1))

    def finish_density(y):
        for x in inner_x:
            for z in range(layers):
                total = total_ref[(x - 1) * count_y + y - 1, z * slots : (z + 1) * slots, :].T
                row = jnp.sum(total, axis=0, keepdims=True) * (2.0 * NORMALISE)
                held = own_ref[x - 1, y - 1, z, 6:7, :] > 0.0
                safe_ref[x - 1, y - 1, z : z + 1, :] = jnp.where(held, row, 1.0)

    if early:
        finish_density(in_order[0])
        start_first()
    pl.when(low_first)(lambda: wait_side(-1, copies))
    pl.when(jnp.logical_not(low_first))(lambda: wait_side(1, copies))
    for x in range(count_x + 2):
        for z in range(layers):
            enter_near(x, other_side, z)
    sweep((pairs_with(high_side), pairs_with(low_side)), span, dist_ref, density_step)
    for y in in_order[1:] if early else in_order:
        finish_density(y)
    if not early:
        start_first()
    start_side(0)
    pl.when(low_first)(lambda: start_side(1))
    pl.when(jnp.logical_not(low_first))(lambda: start_side(-1))
    for copy in copies:
        copy.wait_send()
    for column, (x, y) in enumerate(own):
        for z in range(layers):
            warm = thermal_rows(own_ref[x - 1, y - 1, z, 7:8, :], safe_ref[x - 1, y - 1, z : z + 1, :])
            warm_row_ref[block_of(x, y) * layers + z] = warm
            turned = jnp.concatenate([warm] + [none] * 7, axis=0).T
            for k in range(3):
                mine_ref[column, k, pl.ds(z * slots, slots), :] = jnp.broadcast_to(
                    turned[:, k : k + 1], (slots, slots)
                )
    always, waiting, _ = split_own(own, size_y)
    sweep(always, 2 * span, pair_ref, force_step)
    if waiting:
        pl.when(my_y < 2)(lambda: sweep(waiting, 2 * span, pair_ref, force_step))
    for copy in rho_copies:
        copy.wait()
    halo = across + low_side + high_side
    for x, y in halo:
        for z in range(layers):
            warm = thermal_rows(ext_ref[x, y, z, 7:8, :], near_ref[x, y, z : z + 1, :])
            warm_row_ref[block_of(x, y) * layers + z] = warm


def force_kernel(
    shape, counts_hbm, left_ref, right_ref, near_row_ref, warm_row_ref, mine_ref, start_ref, safe_ref,
    density_out, accel_out, heat_out, counts_ref, sums_ref, pair_ref, table_ref, length_ref, in_sem,
):
    count_x, count_y, layers, slots = shape
    size_y = count_y + 2
    span = layers * slots
    own = [(x, y) for x in range(1, count_x + 1) for y in range(1, count_y + 1)]
    columns = [(x, y) for x in range(count_x + 2) for y in range(size_y)]
    spare = len(columns) * layers
    always, waiting, _ = split_own(own, size_y)
    elsewhere = jnp.where(lax.axis_index("gy") < 2, 0, 1)
    load = pltpu.make_async_copy(counts_hbm, counts_ref, in_sem)
    load.start()
    sums_ref[...] = start_ref[...]
    second = []
    for block in range(len(columns)):
        held = jnp.sum(near_row_ref[block * layers + 1, 6:7, :])
        second.append(jnp.where(held > 0.0, 1, 0))
    for column, (x, y) in enumerate(own):
        length = jnp.int32(0)
        for pair in pairs_between([(x, y)], columns, size_y):
            if (column, pair[1]) not in always:
                table_ref[column, length] = pair[1] * layers
                table_ref[column, length + 1] = pair[1] * layers + 1
                found = 1 + second[pair[1]]
                length = length + (found * elsewhere if (column, pair[1]) in waiting else found)
        for k in range(2 * UNITS):
            table_ref[column, length + k] = spare
        length_ref[column] = length

    load.wait()

    def run(column, count):
        def products(units):
            left = [left_ref[column, first : first + count, 0:DEPTH] for first in (0, span)]
            return multiply(jnp.concatenate(left, axis=0), right_ref, units)

        def keep(found):
            pair_ref[0:count, :] = found[0:count]
            pair_ref[span : span + count, :] = found[count:]

        def units_at(step):
            return tuple(table_ref[column, step * UNITS + k] for k in range(UNITS))

        keep(products(units_at(0)))

        def body(step, carry):
            units, following = carry
            found = products(following)
            add_forces(
                column, units, count, span, near_row_ref, warm_row_ref, mine_ref, pair_ref, sums_ref
            )
            keep(found)
            return following, units_at(jnp.minimum(step + 2, steps))

        steps = (length_ref[column] + (UNITS - 1)) // UNITS
        lax.fori_loop(0, steps, body, (units_at(0), units_at(1)))

    def each(column, carry):
        x, y = column // count_y, lax.rem(column, count_y)
        held = counts_ref[x, y, 0] + counts_ref[x, y, 1]
        for count in range(CHUNK, span + 1, CHUNK):
            pl.when(jnp.logical_and(held > count - CHUNK, held <= count))(functools.partial(run, column, count))
        return carry

    lax.fori_loop(0, len(own), each, 0)
    factor = 1.5 * NORMALISE / SMOOTHING
    rows = lax.broadcasted_iota(jnp.int32, (8, slots), 0)
    lane = lax.broadcasted_iota(jnp.int32, (8, slots), 1)
    for column, (x, y) in enumerate(own):
        packed = []
        for z in range(layers):
            at = slice(z * slots, (z + 1) * slots)
            sums = [jnp.sum(sums_ref[column, k, at, :].T, axis=0, keepdims=True) for k in range(SUMS)]
            unit = (x * size_y + y) * layers + z
            result = jnp.broadcast_to(safe_ref[x - 1, y - 1, z : z + 1, :], (8, slots))
            for f in range(3):
                value = (near_row_ref[unit, f : f + 1, :] * sums[0] - sums[1 + f]) * factor
                result = jnp.where(rows == f, value, result)
            packed.append(jnp.where(rows == 3, sums[4] * (-2.0 * factor), result))
        below = counts_ref[x - 1, y - 1, 0]
        back = jnp.where(below == slots, 0, slots - below)
        lower, upper = pltpu.roll(packed[0], back, 1), pltpu.roll(packed[1], back, 1)
        cells = [packed[0], jnp.where(lane < slots - below, lower, upper)]
        for z in range(layers):
            cell = jnp.where(lane < counts_ref[x - 1, y - 1, z], cells[z], 0.0)
            for f in range(3):
                accel_out[f, x - 1, y - 1, z : z + 1, :] = cell[f : f + 1]
            heat_out[x - 1, y - 1, z : z + 1, :] = cell[3:4]
            density_out[x - 1, y - 1, z : z + 1, :] = cell[4:5]


def shards(offsets, velocity, mass, energy, counts):
    slots = mass.shape[-1]
    count_x, count_y, layers = mass.shape[:3]
    wide_x, wide_y = count_x + 2, count_y + 2
    own = count_x * count_y
    span = layers * slots
    vmem = pl.BlockSpec(memory_space=VMEM)
    units = wide_x * wide_y * layers + 1
    shapes = (mass.shape, (3,) + mass.shape, mass.shape)
    between = [
        VMEM((own, 2 * span, 128), jnp.bfloat16),
        VMEM((units, DEPTH, slots), jnp.bfloat16),
        VMEM((units, 8, slots), jnp.float32),
        VMEM((units, 8, slots), jnp.float32),
        VMEM((own, 3, span, slots), jnp.float32),
        VMEM((own, SUMS, span, slots), jnp.float32),
        VMEM((count_x, count_y, layers, slots), jnp.float32),
    ]
    hbm = pl.BlockSpec(memory_space=pltpu.HBM)
    inputs = [
        pltpu.with_memory_space_constraint(x, pltpu.HBM)
        for x in (offsets, velocity, mass, energy, counts)
    ]
    sems = pltpu.SemaphoreType.DMA((len(DIRECTIONS),))
    cell_shape = (layers, 8, slots)
    results = pl.pallas_call(
        functools.partial(sph_kernel, lax.axis_size("gx"), lax.axis_size("gy")),
        out_shape=between,
        in_specs=[hbm] * 5,
        out_specs=[vmem] * len(between),
        scratch_shapes=[
            VMEM(offsets.shape, jnp.float32),
            VMEM(velocity.shape, jnp.float32),
            VMEM(mass.shape, jnp.float32),
            VMEM(energy.shape, jnp.float32),
            pltpu.SMEM(counts.shape, jnp.int32),
            VMEM((count_x, count_y) + cell_shape, jnp.float32),
            VMEM((wide_x, wide_y) + cell_shape, jnp.float32),
            VMEM((wide_x, wide_y, layers, slots), jnp.float32),
            VMEM((own, span, slots), jnp.float32),
            VMEM((span, span), jnp.float32),
            VMEM((2 * span, span), jnp.float32),
            sems,
            sems,
            sems,
            sems,
            pltpu.SemaphoreType.DMA((5,)),
        ],
        compiler_params=pltpu.CompilerParams(
            collective_id=0, has_side_effects=True, vmem_limit_bytes=VMEM_GRANT
        ),
        name="sph",
    )(*inputs)
    return pl.pallas_call(
        functools.partial(force_kernel, mass.shape),
        out_shape=[jax.ShapeDtypeStruct(shape, jnp.float32) for shape in shapes],
        in_specs=[hbm] + [vmem] * len(between),
        out_specs=[vmem] * 3,
        scratch_shapes=[
            pltpu.SMEM(counts.shape, jnp.int32),
            VMEM((own, SUMS, span, slots), jnp.float32),
            VMEM((2 * span, UNITS * slots), jnp.float32),
            pltpu.SMEM((own, 9 * layers + 2 * UNITS), jnp.int32),
            pltpu.SMEM((own,), jnp.int32),
            pltpu.SemaphoreType.DMA,
        ],
        compiler_params=pltpu.CompilerParams(vmem_limit_bytes=VMEM_GRANT),
        name="force",
    )(inputs[4], *[pltpu.with_memory_space_constraint(result, VMEM) for result in results])


def solution(mesh):
    in_specs = (
        P(None, "gx", "gy", None, None),
        P(None, "gx", "gy", None, None),
        P("gx", "gy", None, None),
        P("gx", "gy", None, None),
        P("gx", "gy", None),
    )
    out_specs = (
        P("gx", "gy", None, None),
        P(None, "gx", "gy", None, None),
        P("gx", "gy", None, None),
    )
    return jax.shard_map(shards, mesh=mesh, in_specs=in_specs, out_specs=out_specs, check_vma=False)
```
